1024 devices in a mesh: atm: 32 (over y_hi, z), cpl: 32 (over x, y_lo, core).
Axes of the slice: x: 8, y: 8 (y_hi: 4, y_lo: 2; y = y_hi * 2 + y_lo), z: 8, core: 2. Of those that a mesh axis runs over, the one named last changes fastest.
Arguments:
- air_temp: float32 [768, 64, 4096], P('atm', None, 'cpl'), may hold values from -6 to 6
- wind_field: bfloat16 [2, 768, 64, 4096], P(None, 'atm', None, 'cpl'), may hold values from -0.3984375 to 0.3984375
- physics: float32 [64, 64], replicated, may hold values from -0.75 to 0.75
- sea_surface: float32 [768, 4096], P('atm', 'cpl'), may hold values from -6 to 6
- shortwave: float32 [768, 4096], P('atm', 'cpl'), may hold values from 0 to 1
- ocean_mask: int32 [768, 4096], P('atm', 'cpl'), may hold values 0 or 1
- owner_route: int32 [32, 768, 1], P('cpl', 'atm'), may hold values from 0 to 31; in each aligned block of 24 rows (0 to 23, 24 to 47, ..., all dimensions but the last counted through in order) at most 2 rows name the same one
- ocean_tile: int32 [32, 768], P('cpl', 'atm'), may hold values from 0 to 23
- weight_tile: int32 [32, 768], P('cpl', 'atm'), may hold values from 0 to 15
- remap_tiles: float32 [16, 32, 128], replicated, may hold values from 0.002 to 0.03
- ocean_temp: float32 [80, 786432], P(None, ('atm', 'cpl')), may hold values from -6 to 6
- mixing: float32 [80, 80], replicated, may hold values from -0.625 to 0.625
Outputs:
- air_next: float32 [768, 64, 4096], P('atm', None, 'cpl')
- ocean_next: float32 [80, 786432], P(None, ('atm', 'cpl'))
- surface_temp: float32 [768, 4096], P('atm', 'cpl')
The draws below stay inside these ranges and needn't reach their ends.
Inputs may be any that keep to these rules, and one draw needn't show every extreme that they name: `owner_route`: among the 24 tiles of one device at most 2 name the same owner, and in every draw some device's tiles name one owner exactly 2 times. `ocean_tile`: ocean tile index within the owner. `weight_tile`: row of remap_tiles used by the tile.
All inputs are finite; a program needn't handle non-finite values. No bound on the sum of `ocean_mask` on one device may be relied on, other than what follows from the above.
Results may differ from the reference program's by a relative error of at most 0.0015.
Values may be sent and summed in bfloat16 or wider, within the bound.
A program may use at most 32 MiB of HBM per device.

```python
import math
import jax
import jax.numpy as jnp
import numpy as np
from jax import lax

GX = 24
GY = 128
LEV = 64
OLEV = 80
WT = 16
OTILE = 32
CAP = 2
NX = 768
NY = 4096
NOCN = 786432
N_ATM = 32
N_CPL = 32


def plant(array, rng, least, largest):
    place = [jax.random.randint(jax.random.fold_in(rng, axis), (), 0, length) for axis, length in enumerate(array.shape)]
    longest = array.shape.index(max(array.shape))
    neighbour = place[:longest] + [(place[longest] + 1) % array.shape[longest]] + place[longest + 1:]
    return array.at[tuple(place)].set(least).at[tuple(neighbour)].set(largest)


def level_of(own_key, shape, shards, least, largest):
    def one(axis_at, parts):
        steps = jax.random.uniform(jax.random.fold_in(jax.random.fold_in(own_key, 6), axis_at), (parts,), jnp.float32, least / len(shards), largest / len(shards))
        return jnp.repeat(jnp.exp(steps), shape[axis_at] // parts).reshape((-1,) + (1,) * (len(shape) - axis_at - 1))

    factor_of = one(*shards[0])
    for cut in shards[1:]:
        factor_of = factor_of * one(*cut)
    return factor_of


def assign_block(key, own, number, rows, count, top, limit, skew):
    sequence = jax.random.permutation(key, count)
    packed, ordinary = portions_of(count, rows * top, limit, skew, True), portions_of(count, rows * top, limit, skew, False)
    places = jnp.arange(count)

    def named(lengths, turn):
        used = int((lengths > 0).sum())
        fixed = max(1, used // 4)
        moved = fixed + (places - fixed + turn * (used - fixed)) % max(1, count - fixed)
        return jnp.zeros((count,), jnp.int32).at[sequence[jnp.where(places < fixed, places, moved)]].set(jnp.asarray(lengths, jnp.int32))

    lengths = jnp.where(number % 4 == 0, named(packed, number // 4), named(ordinary, number - number // 4 - 1))
    mixed = jax.random.permutation(jax.random.fold_in(own, 3), count)
    donor, taker = mixed[0:count // 2 * 2:2], mixed[1:count // 2 * 2:2]
    slack = jnp.minimum(lengths[donor] - 1, limit - lengths[taker]) // 2
    slack = jnp.where((donor == sequence[0]) | (taker == sequence[0]) | (lengths[taker] == 0), 0, jnp.maximum(slack, 0))
    moved = jax.random.randint(jax.random.fold_in(own, 4), (count // 2,), 0, 1 << 20) % (slack + 1)
    lengths = lengths.at[donor].add(-moved).at[taker].add(moved)
    items = jnp.searchsorted(jnp.cumsum(lengths), jnp.arange(rows * top), side="right").astype(jnp.int32)
    listing = items.reshape(top, rows).T
    listing = listing[jax.random.permutation(jax.random.fold_in(own, 1), rows)]
    turn = jax.random.randint(jax.random.fold_in(own, 2), (rows, 1), 0, top)
    return jnp.take_along_axis(listing, (jnp.arange(top)[None, :] + turn) % top, axis=1)


def portions_of(count, total, most, slope, full):
    loads = [(1 << 20) // math.isqrt(grade ** slope) + 1 for grade in range(1, count + 1)]
    largest = most if full else min(most, max(-(-total // count), total * loads[0] // sum(loads)))
    least = 1 if total - largest >= count - 1 else 0
    counts, surplus = [largest] + [least] * (count - 1), total - largest - least * (count - 1)
    while surplus > 0:
        candidates = [i for i in range(1, count) if counts[i] < largest] or [i for i in range(1, count) if counts[i] < most]
        mass, left = sum([loads[i] for i in candidates]), surplus
        for i in candidates:
            more = min(most - counts[i], max(1, left * loads[i] // mass), surplus)
            counts[i] = counts[i] + more
            surplus = surplus - more
    return np.array(counts)


def bell_draw(stream_key, extent, deviation, reach, pieces=(), kind=jnp.bfloat16):
    level = level_of(stream_key, extent, pieces, -0.22, 0.18) if pieces else 1.0
    result = jax.random.normal(stream_key, extent, jnp.float32) * deviation * level
    return jnp.minimum(jnp.maximum(result, -reach), reach).astype(kind)


def setup_inputs(seed: int = 0) -> dict:
    keys = jax.random.split(jax.random.key(seed), 13)
    air_temp = bell_draw(keys[0], (NX, LEV, NY), 1.0, 6.0, ((0, 32), (2, 32)), jnp.float32)
    wind_field = jnp.clip(jax.random.uniform(keys[1], (2, NX, LEV, NY), jnp.float32, -0.3984375, 0.3984375) * level_of(keys[1], (2, NX, LEV, NY), ((1, 32), (3, 32)), -0.4, 0.0), -0.3984375, 0.3984375).astype(jnp.bfloat16)
    physics = bell_draw(keys[2], (LEV, LEV), LEV ** -0.5, 0.75, (), jnp.float32)
    sea_surface = bell_draw(keys[3], (NX, NY), 1.0, 6.0, ((0, 32), (1, 32)), jnp.float32)
    shortwave = jnp.clip(1.0 * jax.random.uniform(keys[4], (NX, NY), jnp.float32) ** level_of(keys[4], (NX, NY), ((0, 32), (1, 32)), -0.2, 0.2), 0.0, 1.0)
    ocean_mask = plant((jax.random.randint(keys[5], (NX, NY), 0, 3) < 2).astype(jnp.int32), jax.random.fold_in(keys[5], 1), 0, 1)
    owner_route_keys = jax.random.split(jax.random.fold_in(keys[6], 1), N_CPL * NX // GX)
    owner_route_turns = jax.random.permutation(jax.random.fold_in(keys[6], 3), N_CPL * NX // GX)
    owner_route = jax.vmap(lambda own, number: assign_block(jax.random.fold_in(keys[6], 2), own, number, GX, N_CPL, 1, CAP, 2))(owner_route_keys, owner_route_turns).reshape((N_CPL, NX, 1))
    ocean_tile = plant(jax.random.randint(keys[7], (N_CPL, NX), 0, GX), jax.random.fold_in(keys[7], 1), 0, GX - 1).astype(jnp.int32)
    weight_tile = plant(jax.random.randint(keys[8], (N_CPL, NX), 0, WT), jax.random.fold_in(keys[8], 1), 0, WT - 1).astype(jnp.int32)
    remap_tiles = jnp.clip(jnp.exp(jax.random.uniform(keys[9], (WT, OTILE, GY), jnp.float32, math.log(0.002), math.log(0.03))), 0.002, 0.03)
    ocean_temp = bell_draw(keys[10], (OLEV, NOCN), 1.0, 6.0, ((1, 1024),), jnp.float32)
    mixing = bell_draw(keys[11], (OLEV, OLEV), OLEV ** -0.5, 0.625, (), jnp.float32)
    return dict(air_temp=air_temp, wind_field=wind_field, physics=physics, sea_surface=sea_surface, shortwave=shortwave, ocean_mask=ocean_mask, owner_route=owner_route, ocean_tile=ocean_tile, weight_tile=weight_tile, remap_tiles=remap_tiles, ocean_temp=ocean_temp, mixing=mixing)


diffusion_rate = 0.05
physics_rate = 0.5
highest = lax.Precision.HIGHEST

def transport(center, west_cell, east_cell, south_cell, north_cell, speed_first, speed_second):
    upwind = jnp.maximum(speed_first, 0.0) * (center - west_cell) + jnp.minimum(speed_first, 0.0) * (east_cell - center)
    upwind = upwind + jnp.maximum(speed_second, 0.0) * (center - south_cell) + jnp.minimum(speed_second, 0.0) * (north_cell - center)
    spread = west_cell + east_cell + south_cell + north_cell - 4.0 * center
    return center - upwind + diffusion_rate * spread

def column_physics(air_field, physics):
    tendency = jnp.einsum('kl,xlz->xkz', physics, air_field, precision=highest)
    return air_field + physics_rate * jnp.tanh(tendency)

def tiles_of(surface_grid):
    return surface_grid.reshape(NX, N_CPL, GY).transpose(1, 0, 2)

def reference(air_temp, wind_field, physics, sea_surface, shortwave, ocean_mask, owner_route, ocean_tile, weight_tile, remap_tiles, ocean_temp, mixing):
    speed_first = wind_field[0].astype(jnp.float32)
    speed_second = wind_field[1].astype(jnp.float32)
    air_field = air_temp
    for step_index in range(2):
        air_field = transport(air_field, jnp.roll(air_field, 1, 0), jnp.roll(air_field, -1, 0), jnp.roll(air_field, 1, 2), jnp.roll(air_field, -1, 2), speed_first, speed_second)
        air_field = column_physics(air_field, physics)
    bottom = air_field[:, 0, :]
    bottom_speed = jnp.sqrt(speed_first[:, 0, :] ** 2 + speed_second[:, 0, :] ** 2 + 0.01)
    ocean_frac = ocean_mask.astype(jnp.float32)
    heat_flux = ocean_frac * (0.5 + 2.0 * bottom_speed) * (bottom - sea_surface)
    solar_flux = ocean_frac * shortwave
    flux_tiles = jnp.stack([tiles_of(heat_flux), tiles_of(solar_flux)], axis=2)
    chosen = jnp.take(remap_tiles, weight_tile, axis=0)
    shares = jnp.einsum('cxoa,cxfa->cxfo', chosen, flux_tiles, precision=highest)
    group_index = jnp.arange(NX, dtype=jnp.int32)[None, :] // GX
    target = ((group_index * N_CPL + owner_route[:, :, 0]) * GX + ocean_tile).astype(jnp.int32)
    per_tile = jax.ops.segment_sum(shares.reshape(N_CPL * NX, 2, OTILE), target.reshape(-1), num_segments=N_ATM * N_CPL * GX)
    forcing = per_tile.transpose(1, 0, 2).reshape(2, NOCN)
    depth_index = jnp.arange(OLEV, dtype=jnp.float32)
    profile = jnp.exp(-depth_index / 8.0)
    profile = profile / jnp.sum(profile)
    heated = ocean_temp + forcing[1][None, :] * profile[:, None]
    heated = heated.at[0].add(forcing[0])
    ocean_next = 0.5 * heated + jnp.dot(mixing, heated, precision=highest, preferred_element_type=jnp.float32)
    surface_tiles = ocean_next[0].reshape(N_ATM * N_CPL * GX, OTILE)[target]
    weighted = jnp.einsum('cxoa,cxo->cxa', chosen, surface_tiles, precision=highest)
    returned = weighted / lax.optimization_barrier(jnp.sum(chosen, axis=2))
    returned = returned.transpose(1, 0, 2).reshape(NX, NY)
    surface_temp = ocean_frac * returned + (1.0 - ocean_frac) * bottom
    return (air_field, ocean_next, surface_temp)
```

```python
import functools
import math

import jax
import jax.numpy as jnp
from jax import lax
from jax.experimental import pallas as pl
from jax.experimental.pallas import tpu as pltpu
from jax.sharding import PartitionSpec as P

diffusion_rate = 0.05
physics_rate = 0.5
f32 = jnp.float32
bf16 = jnp.bfloat16
PEERS = 32
WIDE = 32


def split(value):
    high = value.astype(bf16)
    return high, (value - high.astype(f32)).astype(bf16)


def lanes(shape):
    return lax.broadcasted_iota(jnp.int32, shape, len(shape) - 1)


def subs(shape):
    return lax.broadcasted_iota(jnp.int32, shape, len(shape) - 2)


def dot(left, right):
    return jnp.dot(left, right, preferred_element_type=f32)


def dot3(left_parts, right_parts):
    return (
        dot(left_parts[0], right_parts[0])
        + dot(left_parts[0], right_parts[1])
        + dot(left_parts[1], right_parts[0])
    )


def turn(value, shift):
    return pltpu.roll(value, shift, len(value.shape) - 1)


def transport(center, west, east, south, north, first, second):
    first_up = jnp.maximum(first, 0.0)
    first_down = first - first_up
    second_up = jnp.maximum(second, 0.0)
    second_down = second - second_up
    keep = (1.0 - 4.0 * diffusion_rate) - (first_up - first_down) - (second_up - second_down)
    return (
        center * keep
        + west * (first_up + diffusion_rate)
        + east * (diffusion_rate - first_down)
        + south * (second_up + diffusion_rate)
        + north * (diffusion_rate - second_down)
    )


def kernel(
    groups,
    rings,
    air_hbm,
    wind_hbm,
    physics_ref,
    sea_ref,
    short_ref,
    mask_ref,
    route_ref,
    tile_ref,
    weight_ref,
    remap_ref,
    ocean_hbm,
    mixing_ref,
    air_out,
    ocean_out,
    surface_out,
    air,
    mid,
    last,
    wind,
    parts,
    ocean,
    base,
    base_top,
    bank,
    bank_turned,
    bottom_ref,
    gust_ref,
    surface,
    rows_out,
    rows_in,
    edge_out,
    edge_in,
    info_out,
    info_in,
    flux_out,
    flux_in,
    back_out,
    back_in,
    load_sem,
    store_sem,
    halo_send,
    halo_recv,
    swap_send,
    swap_recv,
):
    rows, levels, width = air_hbm.shape[0], air_hbm.shape[1], air_hbm.shape[2]
    depth = ocean_hbm.shape[0]
    blocks = ocean_hbm.shape[1] // width
    banks = remap_ref.shape[0]
    atm, cpl = lax.axis_index("atm"), lax.axis_index("cpl")
    west = lax.rem(atm + rings - 1, rings)
    east = lax.rem(atm + 1, rings)
    south = lax.rem(cpl + groups - 1, groups)
    north = lax.rem(cpl + 1, groups)

    barrier = pltpu.get_barrier_semaphore()
    for near in (west, east):
        pl.semaphore_signal(barrier, inc=1, device_id={"atm": near, "cpl": cpl})

    def greet(step, carry):
        pl.semaphore_signal(
            barrier, inc=1, device_id={"atm": atm, "cpl": lax.rem(cpl + step, groups)}
        )
        return carry

    lax.fori_loop(1, groups, greet, 0)

    load_air = pltpu.make_async_copy(air_hbm, air.at[pl.ds(1, rows)], load_sem.at[0])
    load_wind = pltpu.make_async_copy(wind_hbm, wind, load_sem.at[1])
    load_ocean = pltpu.make_async_copy(ocean_hbm, ocean, load_sem.at[2])
    load_air.start()
    load_wind.start()
    load_ocean.start()

    if groups < PEERS:
        for unused in (info_in, flux_in, back_in):
            unused[pl.ds(groups, PEERS - groups)] = jnp.zeros(
                (PEERS - groups, 1, width), f32
            )

    sheet = (levels, width)
    lane = lanes(sheet)
    spot = lane % 4
    owner_lane = lane // 4

    square = (rows, width)
    lane_x, sub_x = lanes(square), subs(square)
    route_col = route_ref[0]
    route_all = jnp.broadcast_to(route_col, square).astype(f32)
    diagonal = lane_x % WIDE == sub_x
    route_row = jnp.sum(jnp.where(diagonal, route_all, 0.0), axis=0, keepdims=True)
    same = route_all == route_row
    rank_row = jnp.sum(
        jnp.where(same & (sub_x < lane_x % WIDE), 1.0, 0.0), axis=0, keepdims=True
    )
    rank_col = jnp.sum(
        jnp.where(same & (lane_x < sub_x), 1.0, 0.0), axis=1, keepdims=True
    )
    me = cpl.astype(f32)
    rel_row = route_row - me
    rel_row = jnp.where(rel_row < 0.0, rel_row + groups, rel_row)
    rel_col = route_col.astype(f32) - me
    rel_col = jnp.where(rel_col < 0.0, rel_col + groups, rel_col)
    peer = (PEERS, width)
    lane_p, sub_p = lanes(peer), subs(peer)
    half_p = (lane_p // WIDE) % 2
    placing = jnp.where(
        (rel_row == sub_p.astype(f32))
        & (rank_row == half_p.astype(f32))
        & (lane_p % WIDE < rows),
        1.0,
        0.0,
    ).astype(bf16)
    taking = jnp.where(
        (rank_col * WIDE + rel_col) == (lane_x % (2 * WIDE)).astype(f32), 1.0, 0.0
    ).astype(bf16)
    row_of = lambda ref: jnp.broadcast_to(
        jnp.concatenate(
            [ref[...].astype(f32), jnp.zeros((1, width - rows), f32)], axis=1
        ),
        square,
    )
    column_of = lambda ref: jnp.sum(
        jnp.where(lane_x == sub_x, row_of(ref), 0.0), axis=1, keepdims=True
    )
    tile_col = column_of(tile_ref)
    weight_col = column_of(weight_ref)
    pad_rows = jnp.zeros((WIDE - rows, width), f32)

    def two_halves(value, of_half):
        return [
            jnp.concatenate([jnp.where(of_half == part, value, 0.0), pad_rows], axis=0)
            for part in range(2)
        ]

    tile_all = jnp.broadcast_to(tile_col + 1.0, square)
    info_rows = jnp.concatenate(
        two_halves(tile_all, (lane_x // WIDE) % 2), axis=0
    ).astype(bf16)
    info = dot(placing[:, : 2 * WIDE], info_rows)
    info_out[...] = info.reshape(PEERS, 1, width)
    info_in[pl.ds(0, 1)] = info[0:1].reshape(1, 1, width)

    load_air.wait()
    rows_out[0] = air[1].astype(bf16)
    rows_out[1] = air[rows].astype(bf16)
    load_wind.wait()

    def gather(index, carry):
        columns, first, second = carry
        shift = 4 * index + 6
        mine = owner_lane == index + 1
        columns = jnp.where(mine, turn(air[index + 1], shift), columns)
        one = wind[0, index].astype(f32)
        two = wind[1, index].astype(f32)
        first = jnp.where(mine, turn(one, shift), first)
        second = jnp.where(mine, turn(two, shift), second)
        gust_ref[pl.ds(index, 1), :] = one[0:1] * one[0:1] + two[0:1] * two[0:1]
        return columns, first, second

    empty = jnp.zeros(sheet, f32)
    columns, edge_first, edge_second = lax.fori_loop(
        0, rows, gather, (empty, empty, empty), unroll=4
    )
    edge_out[0] = columns.astype(bf16)

    pl.semaphore_wait(barrier, groups + 1)

    def ring(source, target, slot, device):
        return pltpu.make_async_remote_copy(
            src_ref=source,
            dst_ref=target,
            send_sem=halo_send.at[slot],
            recv_sem=halo_recv.at[slot],
            device_id=device,
        )

    def halo(phase):
        copies = (
            ring(
                rows_out.at[2 * phase],
                rows_in.at[2 * phase],
                4 * phase,
                {"atm": west, "cpl": cpl},
            ),
            ring(
                rows_out.at[2 * phase + 1],
                rows_in.at[2 * phase + 1],
                4 * phase + 1,
                {"atm": east, "cpl": cpl},
            ),
            ring(
                edge_out.at[phase],
                edge_in.at[2 * phase],
                4 * phase + 2,
                {"atm": atm, "cpl": south},
            ),
            ring(
                edge_out.at[phase],
                edge_in.at[2 * phase + 1],
                4 * phase + 3,
                {"atm": atm, "cpl": north},
            ),
        )
        return copies

    def swap(source, target, slot, sign):
        def send(step, carry):
            device = lax.rem(cpl + sign * step + groups, groups)
            pltpu.make_async_remote_copy(
                src_ref=source.at[step],
                dst_ref=target.at[step],
                send_sem=swap_send.at[slot],
                recv_sem=swap_recv.at[slot],
                device_id={"atm": atm, "cpl": device},
            ).start()
            return carry

        lax.fori_loop(1, groups, send, 0)

    def whole(source, target, slot):
        return pltpu.make_async_remote_copy(
            src_ref=source.at[pl.ds(1, groups - 1)],
            dst_ref=target.at[pl.ds(1, groups - 1)],
            send_sem=swap_send.at[slot],
            recv_sem=swap_recv.at[slot],
            device_id={"atm": atm, "cpl": north},
        )

    first_halo = halo(0)
    for copy in first_halo:
        copy.start()
    swap(info_out, info_in, 0, 1)

    physics_parts = split(physics_ref[...])
    physics_wide = jnp.concatenate(
        [physics_parts[0].astype(f32), physics_parts[1].astype(f32)], axis=1
    ).astype(bf16)

    def tendency(high, low):
        return dot(physics_wide, jnp.concatenate([high, high], axis=0)) + dot(
            physics_parts[0], low
        )

    flat = remap_ref[...].reshape(banks * WIDE, width)
    flat_high, flat_low = split(flat)
    bank[0] = flat_high
    bank[1] = flat_low
    turned_high, turned_low = split(jnp.transpose(flat))
    bank_turned[0] = turned_high
    bank_turned[1] = turned_low
    totals = jnp.sum(remap_ref[...], axis=1)
    bank_lane = lanes((rows, banks * WIDE)) // WIDE
    chosen = bank_lane.astype(f32) == weight_col
    pick = jnp.where(
        lanes((rows, banks)).astype(f32) == weight_col, 1.0, 0.0
    )
    inverse = 1.0 / jnp.dot(
        pick, totals, precision=lax.Precision.HIGHEST, preferred_element_type=f32
    )

    def folded(flux):
        high, low = split(flux)
        each = (
            dot(high, bank_turned[0]) + dot(low, bank_turned[0]) + dot(high, bank_turned[1])
        )
        each = jnp.where(chosen, each, 0.0)
        total = each[:, :width]
        for part in range(1, banks * WIDE // width):
            total = total + each[:, part * width : (part + 1) * width]
        total = total + turn(total, WIDE)
        return total + turn(total, 2 * WIDE)

    fraction = mask_ref[...].astype(f32)
    solar_share = folded(fraction * short_ref[...])
    exchange_speed = fraction * (0.5 + 2.0 * jnp.sqrt(gust_ref[...] + 0.01))
    heat_offset = sea_ref[...]

    load_ocean.wait()
    mixing = mixing_ref[...]
    mixing_parts = split(mixing)
    ocean_now = ocean[...]
    base[...] = 0.5 * ocean_now + dot3(mixing_parts, split(ocean_now))
    base_top[...] = jnp.zeros_like(base_top)
    for block in range(blocks):
        base_top[pl.ds(block, 1), :] = base[pl.ds(0, 1), pl.ds(block * width, width)]
    scale = 1.0 / sum(math.exp(-level / 8.0) for level in range(depth))
    profile_row = jnp.exp(lanes((depth, depth)).astype(f32) * -0.125) * scale
    profile_col = jnp.exp(subs((depth, 1)).astype(f32) * -0.125) * scale
    solar_gain = 0.5 * profile_col + jnp.sum(mixing * profile_row, axis=1, keepdims=True)
    heat_gain = mixing[:, 0:1] + jnp.where(subs((depth, 1)) == 0, 0.5, 0.0)
    physics_top = jnp.sum(
        jnp.where(
            lanes((levels, levels)) == subs((levels, levels)), physics_ref[0:1, :], 0.0
        ),
        axis=1,
        keepdims=True,
    )
    physics_top = jnp.broadcast_to(physics_top, sheet)

    def moved(field, sides, index):
        center = field[index + 1]
        fringe = turn(sides, width - (4 * index + 6))
        return transport(
            center,
            field[index],
            field[index + 2],
            turn(jnp.where(lane == width - 1, fringe, center), 1),
            turn(jnp.where(lane == 0, fringe, center), width - 1),
            wind[0, index].astype(f32),
            wind[1, index].astype(f32),
        )

    def arrive(phase, copies, field):
        for copy in copies:
            copy.wait_recv()
        field[rows + 1] = rows_in[2 * phase].astype(f32)
        field[0] = rows_in[2 * phase + 1].astype(f32)
        from_north = edge_in[2 * phase].astype(f32)
        from_south = edge_in[2 * phase + 1].astype(f32)
        return from_south, from_north

    from_south, from_north = arrive(0, first_halo, air)
    sides = jnp.where(spot == 1, from_south, from_north)
    columns = jnp.where(owner_lane == 0, turn(air[0], 2), columns)
    columns = jnp.where(
        owner_lane == rows + 1, turn(air[rows + 1], 4 * rows + 6), columns
    )
    edge = transport(
        columns,
        turn(columns, 4),
        turn(columns, width - 4),
        turn(jnp.where(spot == 1, from_south, columns), 1),
        turn(jnp.where(spot == 2, from_north, columns), width - 1),
        edge_first,
        edge_second,
    )
    ends = [moved(air, sides, 0), moved(air, sides, rows - 1), edge]
    joined = jnp.concatenate(ends, axis=1)
    joined = joined + physics_rate * jnp.tanh(tendency(*split(joined)))
    mid[1] = joined[:, :width]
    mid[rows] = joined[:, width : 2 * width]
    rows_out[2] = joined[:, :width].astype(bf16)
    rows_out[3] = joined[:, width : 2 * width].astype(bf16)
    edge_out[1] = joined[:, 2 * width :].astype(bf16)
    second_halo = halo(1)
    for copy in second_halo:
        copy.start()

    def first_move(index, carry):
        value = moved(air, sides, index)
        high, low = split(value)
        mid[index + 1] = value
        parts[0, index] = high
        parts[1, index] = low
        return carry

    lax.fori_loop(1, rows - 1, first_move, 0, unroll=2)

    def physics_of(field, begin, count):
        high = jnp.concatenate([parts[0, begin + n] for n in range(count)], axis=1)
        low = jnp.concatenate([parts[1, begin + n] for n in range(count)], axis=1)
        change = physics_rate * jnp.tanh(tendency(high, low))
        for n in range(count):
            field[begin + n] = field[begin + n] + change[:, n * width : (n + 1) * width]

    for begin in range(1, rows - 1, 2):
        physics_of(mid.at[pl.ds(1, rows)], begin, 2)

    from_south, from_north = arrive(1, second_halo, mid)
    sides = jnp.where(spot == 1, from_south, from_north)

    def second_move(index, carry):
        value = moved(mid, sides, index)
        high, low = split(value)
        last[index] = value
        parts[0, index] = high
        parts[1, index] = low
        bottom_change = jnp.sum(value * physics_top, axis=0, keepdims=True)
        bottom_ref[pl.ds(index, 1), :] = value[0:1] + physics_rate * jnp.tanh(bottom_change)
        return carry

    lax.fori_loop(0, rows, second_move, 0, unroll=2)

    bottom = bottom_ref[...]
    heat_share = folded(exchange_speed * (bottom - heat_offset))
    share = jnp.where((lane_x // WIDE) % 2 == 0, heat_share, solar_share)
    share_parts = []
    for part in split(share):
        share_parts += two_halves(part.astype(f32), lane_x // (2 * WIDE))
    flux = dot(placing, jnp.concatenate(share_parts, axis=0).astype(bf16))
    flux_out[...] = flux.reshape(PEERS, 1, width)
    flux_in[pl.ds(0, 1)] = flux[0:1].reshape(1, 1, width)
    swap(flux_out, flux_in, 1, 1)

    whole(info_out, info_in, 0).wait_recv()
    tiles_in = info_in[...].reshape(PEERS, width)
    eight = (8, width)
    lane_8, sub_8 = lanes(eight), subs(eight)
    tiles_row = jnp.sum(
        jnp.where(lane_p % WIDE == sub_p, tiles_in, 0.0), axis=0, keepdims=True
    )
    adding = jnp.concatenate(
        [
            jnp.where(
                tiles_row == (4 * sub_8 + 2 * part + lane_8 // (2 * WIDE) + 1).astype(f32),
                1.0,
                0.0,
            )
            for part in range(2)
        ],
        axis=1,
    ).astype(bf16)
    inner = lane_p % WIDE
    reading = jnp.where(
        tiles_in == (4 * (inner % 8) + inner // 8 + 1).astype(f32), 1.0, 0.0
    ).astype(bf16)

    for begin in range(0, rows, 2):
        physics_of(last, begin, 2)
    store_air = pltpu.make_async_copy(last, air_out, store_sem.at[0])
    store_air.start()

    whole(flux_out, flux_in, 1).wait_recv()
    shares_in = flux_in[...].reshape(PEERS, width)
    turned = [turn(shares_in, step * WIDE) if step else shares_in for step in range(4)]
    group_p = lane_p // WIDE
    stacked = []
    for place in range(4):
        here = group_p == place
        for slot in range(2):
            stacked.append(
                jnp.concatenate(
                    [
                        jnp.where(here, turned[(place - 2 * slot - kind) % 4], 0.0)
                        for kind in range(2)
                    ],
                    axis=1,
                )
            )
    stacked = jnp.concatenate(stacked, axis=0)
    stacked_high, stacked_low = split(stacked)
    forcing = dot(adding, stacked_high) + dot(adding, stacked_low)
    heat_in, solar_in = forcing[:, :width], forcing[:, width:]
    top = base_top[...] + solar_gain[0:1] * solar_in + heat_gain[0:1] * heat_in
    spread = []
    for place in range(4):
        mine = jnp.where(lane_8 // WIDE == place, top, 0.0)
        mine = mine + turn(mine, WIDE)
        spread.append(mine + turn(mine, 2 * WIDE))
    spread = jnp.concatenate(spread, axis=0)
    spread_lane = lanes((WIDE, width)) // (2 * WIDE)
    read_parts = []
    for part in split(spread):
        for slot in range(2):
            read_parts.append(jnp.where(spread_lane == slot, part.astype(f32), 0.0))
    back = dot(reading, jnp.concatenate(read_parts, axis=0).astype(bf16))
    back_out[...] = back.reshape(PEERS, 1, width)
    back_in[pl.ds(0, 1)] = back[0:1].reshape(1, 1, width)
    swap(back_out, back_in, 2, -1)

    solar_wide = jnp.broadcast_to(solar_gain, (depth, width))
    heat_wide = jnp.broadcast_to(heat_gain, (depth, width))
    for block in range(blocks):
        at = pl.ds(block * width, width)
        ocean[:, at] = (
            base[:, at]
            + solar_wide * solar_in[block : block + 1]
            + heat_wide * heat_in[block : block + 1]
        )
    store_ocean = pltpu.make_async_copy(ocean, ocean_out, store_sem.at[1])
    store_ocean.start()

    whole(back_out, back_in, 2).wait_recv()
    back_now = back_in[...].reshape(PEERS, width)
    back_turned = turn(back_now, 2 * WIDE)
    low_half = lane_p < 2 * WIDE
    served = jnp.concatenate(
        [
            jnp.where(low_half, back_now, back_turned),
            jnp.where(low_half, back_turned, back_now),
        ],
        axis=0,
    )
    served = jnp.concatenate([part.astype(f32) for part in split(served)], axis=0)
    tile_sst = dot(taking, served.astype(bf16))
    tile_sst = jnp.concatenate([tile_sst] * (banks * WIDE // width), axis=1)
    tile_sst = jnp.where(chosen, tile_sst, 0.0)
    sst_high, sst_low = split(tile_sst)
    returned = inverse * (
        dot(sst_high, bank[0]) + dot(sst_high, bank[1]) + dot(sst_low, bank[0])
    )
    surface[...] = fraction * returned + (1.0 - fraction) * bottom
    store_surface = pltpu.make_async_copy(surface, surface_out, store_sem.at[2])
    store_surface.start()

    for copy in first_halo:
        copy.wait_send()
    for copy in second_halo:
        copy.wait_send()
    whole(info_out, info_in, 0).wait_send()
    whole(flux_out, flux_in, 1).wait_send()
    whole(back_out, back_in, 2).wait_send()
    store_air.wait()
    store_ocean.wait()
    store_surface.wait()


def local(groups, rings, *operands):
    air_temp, remap_tiles, ocean_temp = operands[0], operands[9], operands[10]
    rows, levels, width = air_temp.shape
    banks = remap_tiles.shape[0]
    depth = ocean_temp.shape[0]
    anywhere = pl.BlockSpec(memory_space=pl.ANY)
    inside = pl.BlockSpec(memory_space=pltpu.VMEM)
    message = pltpu.VMEM((PEERS, 1, width), f32)
    return pl.pallas_call(
        functools.partial(kernel, groups, rings),
        out_shape=(
            jax.ShapeDtypeStruct(air_temp.shape, f32),
            jax.ShapeDtypeStruct(ocean_temp.shape, f32),
            jax.ShapeDtypeStruct((rows, width), f32),
        ),
        in_specs=[anywhere, anywhere] + [inside] * 8 + [anywhere, inside],
        out_specs=(anywhere, anywhere, anywhere),
        scratch_shapes=[
            pltpu.VMEM((rows + 2, levels, width), f32),
            pltpu.VMEM((rows + 2, levels, width), f32),
            pltpu.VMEM((rows, levels, width), f32),
            pltpu.VMEM((2, rows, levels, width), bf16),
            pltpu.VMEM((2, rows, levels, width), bf16),
            pltpu.VMEM(ocean_temp.shape, f32),
            pltpu.VMEM(ocean_temp.shape, f32),
            pltpu.VMEM((8, width), f32),
            pltpu.VMEM((2, banks * WIDE, width), bf16),
            pltpu.VMEM((2, width, banks * WIDE), bf16),
            pltpu.VMEM((rows, width), f32),
            pltpu.VMEM((rows, width), f32),
            pltpu.VMEM((rows, width), f32),
            pltpu.VMEM((4, levels, width), bf16),
            pltpu.VMEM((4, levels, width), bf16),
            pltpu.VMEM((2, levels, width), bf16),
            pltpu.VMEM((4, levels, width), bf16),
        ]
        + [message] * 6
        + [
            pltpu.SemaphoreType.DMA((3,)),
            pltpu.SemaphoreType.DMA((3,)),
            pltpu.SemaphoreType.DMA((8,)),
            pltpu.SemaphoreType.DMA((8,)),
            pltpu.SemaphoreType.DMA((3,)),
            pltpu.SemaphoreType.DMA((3,)),
        ],
        compiler_params=pltpu.CompilerParams(
            collective_id=0, has_side_effects=True, vmem_limit_bytes=48 * 1024 * 1024
        ),
    )(*operands)


def solution(mesh):
    placed = (
        P("atm", None, "cpl"),
        P(None, "atm", None, "cpl"),
        P(),
        P("atm", "cpl"),
        P("atm", "cpl"),
        P("atm", "cpl"),
        P("cpl", "atm", None),
        P("cpl", "atm"),
        P("cpl", "atm"),
        P(),
        P(None, ("atm", "cpl")),
        P(),
    )
    return jax.shard_map(
        functools.partial(local, mesh.shape["cpl"], mesh.shape["atm"]),
        mesh=mesh,
        in_specs=placed,
        out_specs=(P("atm", None, "cpl"), P(None, ("atm", "cpl")), P("atm", "cpl")),
        check_vma=False,
    )
```

```python
import functools
import math

import jax
import jax.numpy as jnp
from jax import lax
from jax.experimental import pallas as pl
from jax.experimental.pallas import tpu as pltpu
from jax.sharding import PartitionSpec as P

diffusion_rate = 0.05
physics_rate = 0.5
f32 = jnp.float32
bf16 = jnp.bfloat16
PEERS = 32
WIDE = 32


def split(value):
    high = value.astype(bf16)
    return high, (value - high.astype(f32)).astype(bf16)


def lanes(shape):
    return lax.broadcasted_iota(jnp.int32, shape, len(shape) - 1)


def subs(shape):
    return lax.broadcasted_iota(jnp.int32, shape, len(shape) - 2)


def dot(left, right):
    return jnp.dot(left, right, preferred_element_type=f32)


def dot3(left_parts, right_parts):
    return (
        dot(left_parts[0], right_parts[0])
        + dot(left_parts[0], right_parts[1])
        + dot(left_parts[1], right_parts[0])
    )


def turn(value, shift):
    return pltpu.roll(value, shift, len(value.shape) - 1)


def transport(center, west, east, south, north, first, second):
    first_up = jnp.maximum(first, 0.0)
    first_down = first - first_up
    second_up = jnp.maximum(second, 0.0)
    second_down = second - second_up
    keep = (1.0 - 4.0 * diffusion_rate) - (first_up - first_down) - (second_up - second_down)
    return (
        center * keep
        + west * (first_up + diffusion_rate)
        + east * (diffusion_rate - first_down)
        + south * (second_up + diffusion_rate)
        + north * (diffusion_rate - second_down)
    )


def kernel(
    groups,
    rings,
    air_hbm,
    wind_hbm,
    physics_hbm,
    sea_hbm,
    short_hbm,
    mask_hbm,
    route_hbm,
    tile_hbm,
    weight_hbm,
    remap_hbm,
    ocean_hbm,
    mixing_hbm,
    air_out,
    ocean_out,
    surface_out,
    air,
    mid,
    last,
    wind,
    parts,
    ocean,
    base,
    base_top,
    bank,
    bank_turned,
    bottom_ref,
    gust_ref,
    surface,
    rows_out,
    rows_in,
    edge_out,
    edge_in,
    info_out,
    info_in,
    flux_out,
    flux_in,
    back_out,
    back_in,
    physics_ref,
    sea_ref,
    short_ref,
    mask_ref,
    route_ref,
    tile_ref,
    weight_ref,
    remap_ref,
    mixing_ref,
    load_sem,
    store_sem,
    halo_send,
    halo_recv,
    swap_send,
    swap_recv,
):
    rows, levels, width = air_hbm.shape[0], air_hbm.shape[1], air_hbm.shape[2]
    depth = ocean_hbm.shape[0]
    blocks = ocean_hbm.shape[1] // width
    banks = remap_hbm.shape[0]
    atm, cpl = lax.axis_index("atm"), lax.axis_index("cpl")
    west = lax.rem(atm + rings - 1, rings)
    east = lax.rem(atm + 1, rings)
    south = lax.rem(cpl + groups - 1, groups)
    north = lax.rem(cpl + 1, groups)

    barrier = pltpu.get_barrier_semaphore()
    for near in (west, east):
        pl.semaphore_signal(barrier, inc=1, device_id={"atm": near, "cpl": cpl})

    def greet(step, carry):
        pl.semaphore_signal(
            barrier, inc=1, device_id={"atm": atm, "cpl": lax.rem(cpl + step, groups)}
        )
        return carry

    lax.fori_loop(1, groups, greet, 0)

    pairs = (
        (air_hbm, air.at[pl.ds(1, rows)]),
        (wind_hbm, wind),
        (route_hbm, route_ref),
        (tile_hbm, tile_ref),
        (weight_hbm, weight_ref),
        (remap_hbm, remap_ref),
        (physics_hbm, physics_ref),
        (mask_hbm, mask_ref),
        (short_hbm, short_ref),
        (sea_hbm, sea_ref),
        (mixing_hbm, mixing_ref),
        (ocean_hbm, ocean),
    )
    loads = [
        pltpu.make_async_copy(source, target, load_sem.at[slot])
        for slot, (source, target) in enumerate(pairs)
    ]
    for load in loads:
        load.start()

    if groups < PEERS:
        for unused in (info_in, flux_in, back_in):
            unused[pl.ds(groups, PEERS - groups)] = jnp.zeros(
                (PEERS - groups, 1, width), f32
            )

    sheet = (levels, width)
    lane = lanes(sheet)
    spot = lane % 4
    owner_lane = lane // 4

    loads[0].wait()
    rows_out[0] = air[1].astype(bf16)
    rows_out[1] = air[rows].astype(bf16)

    def gather(index, columns):
        here = turn(air[index + 1], 4 * index + 6)
        return jnp.where(owner_lane == index + 1, here, columns)

    empty = jnp.zeros(sheet, f32)
    columns = lax.fori_loop(0, rows, gather, empty, unroll=8)
    edge_out[0] = columns.astype(bf16)

    pl.semaphore_wait(barrier, groups + 1)

    def ring(source, target, slot, device):
        return pltpu.make_async_remote_copy(
            src_ref=source,
            dst_ref=target,
            send_sem=halo_send.at[slot],
            recv_sem=halo_recv.at[slot],
            device_id=device,
        )

    def halo(phase):
        copies = (
            ring(
                rows_out.at[2 * phase],
                rows_in.at[2 * phase],
                4 * phase,
                {"atm": west, "cpl": cpl},
            ),
            ring(
                rows_out.at[2 * phase + 1],
                rows_in.at[2 * phase + 1],
                4 * phase + 1,
                {"atm": east, "cpl": cpl},
            ),
            ring(
                edge_out.at[phase],
                edge_in.at[2 * phase],
                4 * phase + 2,
                {"atm": atm, "cpl": south},
            ),
            ring(
                edge_out.at[phase],
                edge_in.at[2 * phase + 1],
                4 * phase + 3,
                {"atm": atm, "cpl": north},
            ),
        )
        return copies

    def swap(source, target, slot, sign):
        def send(turn_at, carry):
            step = groups // 2 + (1 - 2 * (turn_at % 2)) * ((turn_at + 1) // 2)
            device = lax.rem(cpl + sign * step + groups, groups)
            pltpu.make_async_remote_copy(
                src_ref=source.at[step],
                dst_ref=target.at[step],
                send_sem=swap_send.at[slot],
                recv_sem=swap_recv.at[slot],
                device_id={"atm": atm, "cpl": device},
            ).start()
            return carry

        lax.fori_loop(0, groups - 1, send, 0)

    def whole(source, target, slot):
        return pltpu.make_async_remote_copy(
            src_ref=source.at[pl.ds(1, groups - 1)],
            dst_ref=target.at[pl.ds(1, groups - 1)],
            send_sem=swap_send.at[slot],
            recv_sem=swap_recv.at[slot],
            device_id={"atm": atm, "cpl": north},
        )

    first_halo = halo(0)
    for copy in first_halo:
        copy.start()
    for load in loads[2:5]:
        load.wait()
    square = (rows, width)
    lane_x, sub_x = lanes(square), subs(square)
    row_of = lambda ref: jnp.broadcast_to(
        jnp.concatenate(
            [ref[...].astype(f32), jnp.zeros((1, width - rows), f32)], axis=1
        ),
        square,
    )
    column_of = lambda ref: jnp.sum(
        jnp.where(lane_x == sub_x, row_of(ref), 0.0), axis=1, keepdims=True
    )
    route_col = column_of(route_ref)
    route_all = jnp.broadcast_to(route_col, square)
    diagonal = lane_x % WIDE == sub_x
    route_row = jnp.sum(jnp.where(diagonal, route_all, 0.0), axis=0, keepdims=True)
    same = route_all == route_row
    rank_row = jnp.sum(
        jnp.where(same & (sub_x < lane_x % WIDE), 1.0, 0.0), axis=0, keepdims=True
    )
    rank_col = jnp.sum(
        jnp.where(same & (lane_x < sub_x), 1.0, 0.0), axis=1, keepdims=True
    )
    me = cpl.astype(f32)
    rel_row = route_row - me
    rel_row = jnp.where(rel_row < 0.0, rel_row + groups, rel_row)
    rel_col = route_col - me
    rel_col = jnp.where(rel_col < 0.0, rel_col + groups, rel_col)
    peer = (PEERS, width)
    lane_p, sub_p = lanes(peer), subs(peer)
    half_p = (lane_p // WIDE) % 2
    placing = jnp.where(
        (rel_row == sub_p.astype(f32))
        & (rank_row == half_p.astype(f32))
        & (lane_p % WIDE < rows),
        1.0,
        0.0,
    ).astype(bf16)
    taking = jnp.where(
        (rank_col * WIDE + rel_col) == (lane_x % (2 * WIDE)).astype(f32), 1.0, 0.0
    ).astype(bf16)
    tile_col = column_of(tile_ref)
    weight_col = column_of(weight_ref)
    pad_rows = jnp.zeros((WIDE - rows, width), f32)

    def two_halves(value, of_half):
        return [
            jnp.concatenate([jnp.where(of_half == part, value, 0.0), pad_rows], axis=0)
            for part in range(2)
        ]

    tile_all = jnp.broadcast_to(tile_col + 1.0, square)
    info_rows = jnp.concatenate(
        two_halves(tile_all, (lane_x // WIDE) % 2), axis=0
    ).astype(bf16)
    info = dot(placing[:, : 2 * WIDE], info_rows)
    info_out[...] = info.reshape(PEERS, 1, width)
    info_in[pl.ds(0, 1)] = info[0:1].reshape(1, 1, width)
    swap(info_out, info_in, 0, 1)

    loads[1].wait()

    def gather_wind(index, carry):
        first, second = carry
        mine = owner_lane == index + 1
        one = wind[0, index].astype(f32)
        two = wind[1, index].astype(f32)
        first = jnp.where(mine, turn(one, 4 * index + 6), first)
        second = jnp.where(mine, turn(two, 4 * index + 6), second)
        gust_ref[pl.ds(index, 1), :] = one[0:1] * one[0:1] + two[0:1] * two[0:1]
        return first, second

    edge_first, edge_second = lax.fori_loop(
        0, rows, gather_wind, (empty, empty), unroll=4
    )

    for load in loads[5:]:
        load.wait()

    physics_parts = split(physics_ref[...])
    physics_wide = jnp.concatenate(
        [physics_parts[0].astype(f32), physics_parts[1].astype(f32)], axis=1
    ).astype(bf16)

    def tendency(high, low):
        return dot(physics_wide, jnp.concatenate([high, high], axis=0)) + dot(
            physics_parts[0], low
        )

    flat = remap_ref[...].reshape(banks * WIDE, width)
    flat_high, flat_low = split(flat)
    bank[0] = flat_high
    bank[1] = flat_low
    turned_high, turned_low = split(jnp.transpose(flat))
    bank_turned[0] = turned_high
    bank_turned[1] = turned_low
    totals = jnp.sum(remap_ref[...], axis=1)
    bank_lane = lanes((rows, banks * WIDE)) // WIDE
    chosen = bank_lane.astype(f32) == weight_col
    pick = jnp.where(
        lanes((rows, banks)).astype(f32) == weight_col, 1.0, 0.0
    )
    inverse = 1.0 / jnp.dot(
        pick, totals, precision=lax.Precision.HIGHEST, preferred_element_type=f32
    )

    def folded(flux):
        high, low = split(flux)
        each = (
            dot(high, bank_turned[0]) + dot(low, bank_turned[0]) + dot(high, bank_turned[1])
        )
        each = jnp.where(chosen, each, 0.0)
        total = each[:, :width]
        for part in range(1, banks * WIDE // width):
            total = total + each[:, part * width : (part + 1) * width]
        total = total + turn(total, WIDE)
        return total + turn(total, 2 * WIDE)

    fraction = mask_ref[...].astype(f32)
    solar_share = folded(fraction * short_ref[...])
    exchange_speed = fraction * (0.5 + 2.0 * jnp.sqrt(gust_ref[...] + 0.01))
    heat_offset = sea_ref[...]

    mixing = mixing_ref[...]
    mixing_parts = split(mixing)
    ocean_now = ocean[...]
    base[...] = 0.5 * ocean_now + dot3(mixing_parts, split(ocean_now))
    base_top[...] = jnp.zeros_like(base_top)
    for block in range(blocks):
        base_top[pl.ds(block, 1), :] = base[pl.ds(0, 1), pl.ds(block * width, width)]
    scale = 1.0 / sum(math.exp(-level / 8.0) for level in range(depth))
    profile_row = jnp.exp(lanes((depth, depth)).astype(f32) * -0.125) * scale
    profile_col = jnp.exp(subs((depth, 1)).astype(f32) * -0.125) * scale
    solar_gain = 0.5 * profile_col + jnp.sum(mixing * profile_row, axis=1, keepdims=True)
    heat_gain = mixing[:, 0:1] + jnp.where(subs((depth, 1)) == 0, 0.5, 0.0)
    physics_top = jnp.sum(
        jnp.where(
            lanes((levels, levels)) == subs((levels, levels)), physics_ref[0:1, :], 0.0
        ),
        axis=1,
        keepdims=True,
    )
    physics_top = jnp.broadcast_to(physics_top, sheet)

    def moved(field, sides, index):
        center = field[index + 1]
        fringe = turn(sides, width - (4 * index + 6))
        return transport(
            center,
            field[index],
            field[index + 2],
            turn(jnp.where(lane == width - 1, fringe, center), 1),
            turn(jnp.where(lane == 0, fringe, center), width - 1),
            wind[0, index].astype(f32),
            wind[1, index].astype(f32),
        )

    def arrive(phase, copies, field):
        for copy in copies:
            copy.wait_recv()
        field[rows + 1] = rows_in[2 * phase].astype(f32)
        field[0] = rows_in[2 * phase + 1].astype(f32)
        from_north = edge_in[2 * phase].astype(f32)
        from_south = edge_in[2 * phase + 1].astype(f32)
        return from_south, from_north

    from_south, from_north = arrive(0, first_halo, air)
    sides = jnp.where(spot == 1, from_south, from_north)
    columns = jnp.where(owner_lane == 0, turn(air[0], 2), columns)
    columns = jnp.where(
        owner_lane == rows + 1, turn(air[rows + 1], 4 * rows + 6), columns
    )
    edge = transport(
        columns,
        turn(columns, 4),
        turn(columns, width - 4),
        turn(jnp.where(spot == 1, from_south, columns), 1),
        turn(jnp.where(spot == 2, from_north, columns), width - 1),
        edge_first,
        edge_second,
    )
    ends = [moved(air, sides, 0), moved(air, sides, rows - 1), edge]
    joined = jnp.concatenate(ends, axis=1)
    joined = joined + physics_rate * jnp.tanh(tendency(*split(joined)))
    mid[1] = joined[:, :width]
    mid[rows] = joined[:, width : 2 * width]
    rows_out[2] = joined[:, :width].astype(bf16)
    rows_out[3] = joined[:, width : 2 * width].astype(bf16)
    edge_out[1] = joined[:, 2 * width :].astype(bf16)
    second_halo = halo(1)
    for copy in second_halo:
        copy.start()

    def first_move(index, carry):
        value = moved(air, sides, index)
        high, low = split(value)
        mid[index + 1] = value
        parts[0, index] = high
        parts[1, index] = low
        return carry

    lax.fori_loop(1, rows - 1, first_move, 0, unroll=2)

    def physics_of(field, begin, count):
        high = jnp.concatenate([parts[0, begin + n] for n in range(count)], axis=1)
        low = jnp.concatenate([parts[1, begin + n] for n in range(count)], axis=1)
        change = physics_rate * jnp.tanh(tendency(high, low))
        for n in range(count):
            field[begin + n] = field[begin + n] + change[:, n * width : (n + 1) * width]

    for begin in range(1, rows - 1, 2):
        physics_of(mid.at[pl.ds(1, rows)], begin, 2)

    from_south, from_north = arrive(1, second_halo, mid)
    sides = jnp.where(spot == 1, from_south, from_north)

    def second_move(index, carry):
        value = moved(mid, sides, index)
        high, low = split(value)
        last[index] = value
        parts[0, index] = high
        parts[1, index] = low
        bottom_change = jnp.sum(value * physics_top, axis=0, keepdims=True)
        bottom_ref[pl.ds(index, 1), :] = value[0:1] + physics_rate * jnp.tanh(bottom_change)
        return carry

    lax.fori_loop(0, rows, second_move, 0, unroll=2)

    bottom = bottom_ref[...]
    heat_share = folded(exchange_speed * (bottom - heat_offset))
    share = jnp.where((lane_x // WIDE) % 2 == 0, heat_share, solar_share)
    share_parts = []
    for part in split(share):
        share_parts += two_halves(part.astype(f32), lane_x // (2 * WIDE))
    flux = dot(placing, jnp.concatenate(share_parts, axis=0).astype(bf16))
    flux_out[...] = flux.reshape(PEERS, 1, width)
    flux_in[pl.ds(0, 1)] = flux[0:1].reshape(1, 1, width)
    swap(flux_out, flux_in, 1, 1)

    whole(info_out, info_in, 0).wait_recv()
    tiles_in = info_in[...].reshape(PEERS, width)
    eight = (8, width)
    lane_8, sub_8 = lanes(eight), subs(eight)
    tiles_row = jnp.sum(
        jnp.where(lane_p % WIDE == sub_p, tiles_in, 0.0), axis=0, keepdims=True
    )
    adding = jnp.concatenate(
        [
            jnp.where(
                tiles_row == (4 * sub_8 + 2 * part + lane_8 // (2 * WIDE) + 1).astype(f32),
                1.0,
                0.0,
            )
            for part in range(2)
        ],
        axis=1,
    ).astype(bf16)
    inner = lane_p % WIDE
    reading = jnp.where(
        tiles_in == (4 * (inner % 8) + inner // 8 + 1).astype(f32), 1.0, 0.0
    ).astype(bf16)

    for begin in range(0, rows, 2):
        physics_of(last, begin, 2)
    store_air = pltpu.make_async_copy(last, air_out, store_sem.at[0])
    store_air.start()

    whole(flux_out, flux_in, 1).wait_recv()
    shares_in = flux_in[...].reshape(PEERS, width)
    turned = [turn(shares_in, step * WIDE) if step else shares_in for step in range(4)]
    group_p = lane_p // WIDE
    stacked = []
    for place in range(4):
        here = group_p == place
        for slot in range(2):
            stacked.append(
                jnp.concatenate(
                    [
                        jnp.where(here, turned[(place - 2 * slot - kind) % 4], 0.0)
                        for kind in range(2)
                    ],
                    axis=1,
                )
            )
    stacked = jnp.concatenate(stacked, axis=0)
    stacked_high, stacked_low = split(stacked)
    forcing = dot(adding, stacked_high) + dot(adding, stacked_low)
    heat_in, solar_in = forcing[:, :width], forcing[:, width:]
    top = base_top[...] + solar_gain[0:1] * solar_in + heat_gain[0:1] * heat_in
    spread = []
    for place in range(4):
        mine = jnp.where(lane_8 // WIDE == place, top, 0.0)
        mine = mine + turn(mine, WIDE)
        spread.append(mine + turn(mine, 2 * WIDE))
    spread = jnp.concatenate(spread, axis=0)
    spread_lane = lanes((WIDE, width)) // (2 * WIDE)
    read_parts = []
    for part in split(spread):
        for slot in range(2):
            read_parts.append(jnp.where(spread_lane == slot, part.astype(f32), 0.0))
    back = dot(reading, jnp.concatenate(read_parts, axis=0).astype(bf16))
    back_out[...] = back.reshape(PEERS, 1, width)
    back_in[pl.ds(0, 1)] = back[0:1].reshape(1, 1, width)
    swap(back_out, back_in, 2, -1)

    solar_wide = jnp.broadcast_to(solar_gain, (depth, width))
    heat_wide = jnp.broadcast_to(heat_gain, (depth, width))
    for block in range(blocks):
        at = pl.ds(block * width, width)
        ocean[:, at] = (
            base[:, at]
            + solar_wide * solar_in[block : block + 1]
            + heat_wide * heat_in[block : block + 1]
        )
    store_ocean = pltpu.make_async_copy(ocean, ocean_out, store_sem.at[1])
    store_ocean.start()

    whole(back_out, back_in, 2).wait_recv()
    back_now = back_in[...].reshape(PEERS, width)
    back_turned = turn(back_now, 2 * WIDE)
    low_half = lane_p < 2 * WIDE
    served = jnp.concatenate(
        [
            jnp.where(low_half, back_now, back_turned),
            jnp.where(low_half, back_turned, back_now),
        ],
        axis=0,
    )
    served = jnp.concatenate([part.astype(f32) for part in split(served)], axis=0)
    tile_sst = dot(taking, served.astype(bf16))
    tile_sst = jnp.concatenate([tile_sst] * (banks * WIDE // width), axis=1)
    tile_sst = jnp.where(chosen, tile_sst, 0.0)
    sst_high, sst_low = split(tile_sst)
    returned = inverse * (
        dot(sst_high, bank[0]) + dot(sst_high, bank[1]) + dot(sst_low, bank[0])
    )
    surface[...] = fraction * returned + (1.0 - fraction) * bottom
    store_surface = pltpu.make_async_copy(surface, surface_out, store_sem.at[2])
    store_surface.start()

    for copy in first_halo:
        copy.wait_send()
    for copy in second_halo:
        copy.wait_send()
    whole(info_out, info_in, 0).wait_send()
    whole(flux_out, flux_in, 1).wait_send()
    whole(back_out, back_in, 2).wait_send()
    store_air.wait()
    store_ocean.wait()
    store_surface.wait()


def deliver(air_in, ocean_in, surface_in, air_out, ocean_out, surface_out, sems):
    copies = [
        pltpu.make_async_copy(source, target, sems.at[slot])
        for slot, (source, target) in enumerate(
            ((air_in, air_out), (ocean_in, ocean_out), (surface_in, surface_out))
        )
    ]
    for copy in copies:
        copy.start()
    for copy in copies:
        copy.wait()


def local(groups, rings, *operands):
    route = operands[6]
    operands = operands[:6] + (route.reshape(route.shape[:2]),) + operands[7:]
    air_temp, remap_tiles, ocean_temp = operands[0], operands[9], operands[10]
    rows, levels, width = air_temp.shape
    banks = remap_tiles.shape[0]
    depth = ocean_temp.shape[0]
    anywhere = pl.BlockSpec(memory_space=pl.ANY)
    pinned = pl.BlockSpec(memory_space=pltpu.HBM)
    message = pltpu.VMEM((PEERS, 1, width), f32)
    results = pl.pallas_call(
        functools.partial(kernel, groups, rings),
        out_shape=(
            jax.ShapeDtypeStruct(air_temp.shape, f32),
            jax.ShapeDtypeStruct(ocean_temp.shape, f32),
            jax.ShapeDtypeStruct((rows, width), f32),
        ),
        in_specs=[pinned] * 12,
        out_specs=(anywhere, anywhere, anywhere),
        scratch_shapes=[
            pltpu.VMEM((rows + 2, levels, width), f32),
            pltpu.VMEM((rows + 2, levels, width), f32),
            pltpu.VMEM((rows, levels, width), f32),
            pltpu.VMEM((2, rows, levels, width), bf16),
            pltpu.VMEM((2, rows, levels, width), bf16),
            pltpu.VMEM(ocean_temp.shape, f32),
            pltpu.VMEM(ocean_temp.shape, f32),
            pltpu.VMEM((8, width), f32),
            pltpu.VMEM((2, banks * WIDE, width), bf16),
            pltpu.VMEM((2, width, banks * WIDE), bf16),
            pltpu.VMEM((rows, width), f32),
            pltpu.VMEM((rows, width), f32),
            pltpu.VMEM((rows, width), f32),
            pltpu.VMEM((4, levels, width), bf16),
            pltpu.VMEM((4, levels, width), bf16),
            pltpu.VMEM((2, levels, width), bf16),
            pltpu.VMEM((4, levels, width), bf16),
        ]
        + [message] * 6
        + [
            pltpu.VMEM(operand.shape, operand.dtype)
            for operand in operands[2:10] + operands[11:]
        ]
        + [
            pltpu.SemaphoreType.DMA((12,)),
            pltpu.SemaphoreType.DMA((3,)),
            pltpu.SemaphoreType.DMA((8,)),
            pltpu.SemaphoreType.DMA((8,)),
            pltpu.SemaphoreType.DMA((3,)),
            pltpu.SemaphoreType.DMA((3,)),
        ],
        compiler_params=pltpu.CompilerParams(
            collective_id=0, has_side_effects=True, vmem_limit_bytes=48 * 1024 * 1024
        ),
    )(*[pltpu.with_memory_space_constraint(each, pltpu.HBM) for each in operands])
    return pl.pallas_call(
        deliver,
        out_shape=tuple(jax.ShapeDtypeStruct(each.shape, each.dtype) for each in results),
        in_specs=[anywhere] * 3,
        out_specs=(pinned,) * 3,
        scratch_shapes=[pltpu.SemaphoreType.DMA((3,))],
        compiler_params=pltpu.CompilerParams(vmem_limit_bytes=4 * 1024 * 1024),
    )(*results)


def solution(mesh):
    placed = (
        P("atm", None, "cpl"),
        P(None, "atm", None, "cpl"),
        P(),
        P("atm", "cpl"),
        P("atm", "cpl"),
        P("atm", "cpl"),
        P("cpl", "atm", None),
        P("cpl", "atm"),
        P("cpl", "atm"),
        P(),
        P(None, ("atm", "cpl")),
        P(),
    )
    return jax.shard_map(
        functools.partial(local, mesh.shape["cpl"], mesh.shape["atm"]),
        mesh=mesh,
        in_specs=placed,
        out_specs=(P("atm", None, "cpl"), P(None, ("atm", "cpl")), P("atm", "cpl")),
        check_vma=False,
    )
```

```python
import functools
import math

import jax
import jax.numpy as jnp
from jax import lax
from jax.experimental import pallas as pl
from jax.experimental.pallas import tpu as pltpu
from jax.sharding import PartitionSpec as P

diffusion_rate = 0.05
physics_rate = 0.5
f32 = jnp.float32
bf16 = jnp.bfloat16
PEERS = 32
WIDE = 32


def split(value):
    high = value.astype(bf16)
    return high, (value - high.astype(f32)).astype(bf16)


def lanes(shape):
    return lax.broadcasted_iota(jnp.int32, shape, len(shape) - 1)


def subs(shape):
    return lax.broadcasted_iota(jnp.int32, shape, len(shape) - 2)


def dot(left, right):
    return jnp.dot(left, right, preferred_element_type=f32)


def dot3(left_parts, right_parts):
    return (
        dot(left_parts[0], right_parts[0])
        + dot(left_parts[0], right_parts[1])
        + dot(left_parts[1], right_parts[0])
    )


def turn(value, shift):
    return pltpu.roll(value, shift, len(value.shape) - 1)


def transport(center, west, east, south, north, first, second):
    first_up = jnp.maximum(first, 0.0)
    first_down = first - first_up
    second_up = jnp.maximum(second, 0.0)
    second_down = second - second_up
    keep = (1.0 - 4.0 * diffusion_rate) - (first_up - first_down) - (second_up - second_down)
    return (
        center * keep
        + west * (first_up + diffusion_rate)
        + east * (diffusion_rate - first_down)
        + south * (second_up + diffusion_rate)
        + north * (diffusion_rate - second_down)
    )


def kernel(
    groups,
    rings,
    air_hbm,
    wind_hbm,
    physics_hbm,
    sea_hbm,
    short_hbm,
    mask_hbm,
    route_hbm,
    tile_hbm,
    weight_hbm,
    remap_hbm,
    ocean_hbm,
    mixing_hbm,
    air_out,
    ocean_out,
    surface_out,
    air,
    mid,
    last,
    wind,
    parts,
    ocean,
    base,
    base_top,
    bank,
    bank_turned,
    bottom_ref,
    gust_ref,
    top_ref,
    surface,
    rows_out,
    rows_in,
    edge_out,
    edge_in,
    info_out,
    info_in,
    flux_out,
    flux_in,
    back_out,
    back_in,
    physics_ref,
    sea_ref,
    short_ref,
    mask_ref,
    route_ref,
    tile_ref,
    weight_ref,
    remap_ref,
    mixing_ref,
    load_sem,
    store_sem,
    halo_send,
    halo_recv,
    swap_send,
    swap_recv,
):
    rows, levels, width = air_hbm.shape[0], air_hbm.shape[1], air_hbm.shape[2]
    depth = ocean_hbm.shape[0]
    blocks = ocean_hbm.shape[1] // width
    banks = remap_hbm.shape[0]
    atm, cpl = lax.axis_index("atm"), lax.axis_index("cpl")
    west = lax.rem(atm + rings - 1, rings)
    east = lax.rem(atm + 1, rings)
    south = lax.rem(cpl + groups - 1, groups)
    north = lax.rem(cpl + 1, groups)

    barrier = pltpu.get_barrier_semaphore()
    for near in (west, east):
        pl.semaphore_signal(barrier, inc=1, device_id={"atm": near, "cpl": cpl})

    pairs = (
        (air_hbm, air.at[pl.ds(1, rows)]),
        (wind_hbm, wind),
        (route_hbm, route_ref),
        (tile_hbm, tile_ref),
        (weight_hbm, weight_ref),
        (remap_hbm, remap_ref),
        (physics_hbm, physics_ref),
        (mask_hbm, mask_ref),
        (short_hbm, short_ref),
        (sea_hbm, sea_ref),
        (mixing_hbm, mixing_ref),
        (ocean_hbm, ocean),
    )
    loads = [
        pltpu.make_async_copy(source, target, load_sem.at[slot])
        for slot, (source, target) in enumerate(pairs)
    ]
    loads[0].start()

    def far_first(turn_at):
        return groups // 2 + (1 - 2 * (turn_at % 2)) * ((turn_at + 1) // 2)

    def greet(turn_at, carry):
        peer_at = lax.rem(cpl + far_first(turn_at), groups)
        pl.semaphore_signal(barrier, inc=1, device_id={"atm": atm, "cpl": peer_at})
        return carry

    lax.fori_loop(0, groups - 1, greet, 0)
    for load in loads[1:]:
        load.start()

    if groups < PEERS:
        for unused in (info_in, flux_in, back_in):
            unused[pl.ds(groups, PEERS - groups)] = jnp.zeros(
                (PEERS - groups, 1, width), f32
            )

    sheet = (levels, width)
    lane = lanes(sheet)
    spot = lane % 4
    owner_lane = lane // 4

    loads[0].wait()
    rows_out[0] = air[1].astype(bf16)
    rows_out[1] = air[rows].astype(bf16)

    def gather(index, columns):
        here = turn(air[index + 1], 4 * index + 6)
        return jnp.where(owner_lane == index + 1, here, columns)

    empty = jnp.zeros(sheet, f32)
    columns = lax.fori_loop(0, rows, gather, empty, unroll=8)
    edge_out[0] = columns.astype(bf16)

    pl.semaphore_wait(barrier, groups + 1)

    def ring(source, target, slot, device):
        return pltpu.make_async_remote_copy(
            src_ref=source,
            dst_ref=target,
            send_sem=halo_send.at[slot],
            recv_sem=halo_recv.at[slot],
            device_id=device,
        )

    def halo(phase):
        copies = (
            ring(
                rows_out.at[2 * phase],
                rows_in.at[2 * phase],
                4 * phase,
                {"atm": west, "cpl": cpl},
            ),
            ring(
                rows_out.at[2 * phase + 1],
                rows_in.at[2 * phase + 1],
                4 * phase + 1,
                {"atm": east, "cpl": cpl},
            ),
            ring(
                edge_out.at[phase],
                edge_in.at[2 * phase],
                4 * phase + 2,
                {"atm": atm, "cpl": south},
            ),
            ring(
                edge_out.at[phase],
                edge_in.at[2 * phase + 1],
                4 * phase + 3,
                {"atm": atm, "cpl": north},
            ),
        )
        return copies

    def swap(source, target, slot, sign):
        def send(turn_at, carry):
            step = far_first(turn_at)
            device = lax.rem(cpl + sign * step + groups, groups)
            pltpu.make_async_remote_copy(
                src_ref=source.at[step],
                dst_ref=target.at[step],
                send_sem=swap_send.at[slot],
                recv_sem=swap_recv.at[slot],
                device_id={"atm": atm, "cpl": device},
            ).start()
            return carry

        lax.fori_loop(0, groups - 1, send, 0)

    def whole(source, target, slot):
        return pltpu.make_async_remote_copy(
            src_ref=source.at[pl.ds(1, groups - 1)],
            dst_ref=target.at[pl.ds(1, groups - 1)],
            send_sem=swap_send.at[slot],
            recv_sem=swap_recv.at[slot],
            device_id={"atm": atm, "cpl": north},
        )

    first_halo = halo(0)
    for copy in first_halo:
        copy.start()
    for load in loads[2:5]:
        load.wait()
    square = (rows, width)
    lane_x, sub_x = lanes(square), subs(square)
    row_of = lambda ref: jnp.broadcast_to(
        jnp.concatenate(
            [ref[...].astype(f32), jnp.zeros((1, width - rows), f32)], axis=1
        ),
        square,
    )
    column_of = lambda ref: jnp.sum(
        jnp.where(lane_x == sub_x, row_of(ref), 0.0), axis=1, keepdims=True
    )
    route_col = column_of(route_ref)
    route_all = jnp.broadcast_to(route_col, square)
    diagonal = lane_x % WIDE == sub_x
    route_row = jnp.sum(jnp.where(diagonal, route_all, 0.0), axis=0, keepdims=True)
    same = route_all == route_row
    rank_row = jnp.sum(
        jnp.where(same & (sub_x < lane_x % WIDE), 1.0, 0.0), axis=0, keepdims=True
    )
    rank_col = jnp.sum(
        jnp.where(same & (lane_x < sub_x), 1.0, 0.0), axis=1, keepdims=True
    )
    me = cpl.astype(f32)
    rel_row = route_row - me
    rel_row = jnp.where(rel_row < 0.0, rel_row + groups, rel_row)
    rel_col = route_col - me
    rel_col = jnp.where(rel_col < 0.0, rel_col + groups, rel_col)
    peer = (PEERS, width)
    lane_p, sub_p = lanes(peer), subs(peer)
    half_p = (lane_p // WIDE) % 2
    placing = jnp.where(
        (rel_row == sub_p.astype(f32))
        & (rank_row == half_p.astype(f32))
        & (lane_p % WIDE < rows),
        1.0,
        0.0,
    ).astype(bf16)
    taking = jnp.where(
        (rank_col * WIDE + rel_col) == (lane_x % (2 * WIDE)).astype(f32), 1.0, 0.0
    ).astype(bf16)
    tile_col = column_of(tile_ref)
    weight_col = column_of(weight_ref)
    pad_rows = jnp.zeros((WIDE - rows, width), f32)

    def two_halves(value, of_half):
        return [
            jnp.concatenate([jnp.where(of_half == part, value, 0.0), pad_rows], axis=0)
            for part in range(2)
        ]

    tile_all = jnp.broadcast_to(tile_col + 1.0, square)
    info_rows = jnp.concatenate(
        two_halves(tile_all, (lane_x // WIDE) % 2), axis=0
    ).astype(bf16)
    info = dot(placing[:, : 2 * WIDE], info_rows)
    info_out[...] = info.reshape(PEERS, 1, width)
    info_in[pl.ds(0, 1)] = info[0:1].reshape(1, 1, width)
    swap(info_out, info_in, 0, 1)

    loads[1].wait()

    def gather_wind(index, carry):
        first, second = carry
        mine = owner_lane == index + 1
        one = wind[0, index].astype(f32)
        two = wind[1, index].astype(f32)
        first = jnp.where(mine, turn(one, 4 * index + 6), first)
        second = jnp.where(mine, turn(two, 4 * index + 6), second)
        gust_ref[pl.ds(index, 1), :] = one[0:1] * one[0:1] + two[0:1] * two[0:1]
        return first, second

    edge_first, edge_second = lax.fori_loop(
        0, rows, gather_wind, (empty, empty), unroll=4
    )

    for load in loads[5:]:
        load.wait()

    physics_parts = split(physics_ref[...])
    physics_wide = jnp.concatenate(
        [physics_parts[0].astype(f32), physics_parts[1].astype(f32)], axis=1
    ).astype(bf16)

    def tendency(high, low):
        return dot(physics_wide, jnp.concatenate([high, high], axis=0)) + dot(
            physics_parts[0], low
        )

    flat = remap_ref[...].reshape(banks * WIDE, width)
    flat_high, flat_low = split(flat)
    bank[0] = flat_high
    bank[1] = flat_low
    turned_high, turned_low = split(jnp.transpose(flat))
    bank_turned[0] = turned_high
    bank_turned[1] = turned_low
    totals = jnp.sum(remap_ref[...], axis=1)
    bank_lane = lanes((rows, banks * WIDE)) // WIDE
    chosen = bank_lane.astype(f32) == weight_col
    pick = jnp.where(
        lanes((rows, banks)).astype(f32) == weight_col, 1.0, 0.0
    )
    inverse = 1.0 / jnp.dot(
        pick, totals, precision=lax.Precision.HIGHEST, preferred_element_type=f32
    )

    def folded(flux):
        high, low = split(flux)
        each = (
            dot(high, bank_turned[0]) + dot(low, bank_turned[0]) + dot(high, bank_turned[1])
        )
        each = jnp.where(chosen, each, 0.0)
        total = each[:, :width]
        for part in range(1, banks * WIDE // width):
            total = total + each[:, part * width : (part + 1) * width]
        total = total + turn(total, WIDE)
        return total + turn(total, 2 * WIDE)

    fraction = mask_ref[...].astype(f32)
    solar_share = folded(fraction * short_ref[...])
    exchange_speed = fraction * (0.5 + 2.0 * jnp.sqrt(gust_ref[...] + 0.01))
    heat_offset = sea_ref[...]

    mixing = mixing_ref[...]
    mixing_parts = split(mixing)
    ocean_now = ocean[...]
    base[...] = 0.5 * ocean_now + dot3(mixing_parts, split(ocean_now))
    base_top[...] = jnp.zeros_like(base_top)
    for block in range(blocks):
        base_top[pl.ds(block, 1), :] = base[pl.ds(0, 1), pl.ds(block * width, width)]
    scale = 1.0 / sum(math.exp(-level / 8.0) for level in range(depth))
    profile_row = jnp.exp(lanes((depth, depth)).astype(f32) * -0.125) * scale
    profile_col = jnp.exp(subs((depth, 1)).astype(f32) * -0.125) * scale
    solar_gain = 0.5 * profile_col + jnp.sum(mixing * profile_row, axis=1, keepdims=True)
    heat_gain = mixing[:, 0:1] + jnp.where(subs((depth, 1)) == 0, 0.5, 0.0)
    physics_top = jnp.sum(
        jnp.where(
            lanes((levels, levels)) == subs((levels, levels)), physics_ref[0:1, :], 0.0
        ),
        axis=1,
        keepdims=True,
    )
    physics_top = jnp.broadcast_to(physics_top, sheet)

    def moved(field, sides, index):
        center = field[index + 1]
        fringe = turn(sides, width - (4 * index + 6))
        return transport(
            center,
            field[index],
            field[index + 2],
            turn(jnp.where(lane == width - 1, fringe, center), 1),
            turn(jnp.where(lane == 0, fringe, center), width - 1),
            wind[0, index].astype(f32),
            wind[1, index].astype(f32),
        )

    def arrive(phase, copies):
        for copy in copies:
            copy.wait_recv()
        return (
            rows_in[2 * phase + 1].astype(f32),
            rows_in[2 * phase].astype(f32),
            edge_in[2 * phase + 1].astype(f32),
            edge_in[2 * phase].astype(f32),
        )

    from_west, from_east, from_south, from_north = arrive(0, first_halo)
    air[0] = from_west
    air[rows + 1] = from_east
    sides = jnp.where(spot == 1, from_south, from_north)
    columns = jnp.where(owner_lane == 0, turn(air[0], 2), columns)
    columns = jnp.where(
        owner_lane == rows + 1, turn(air[rows + 1], 4 * rows + 6), columns
    )
    edge = transport(
        columns,
        turn(columns, 4),
        turn(columns, width - 4),
        turn(jnp.where(spot == 1, from_south, columns), 1),
        turn(jnp.where(spot == 2, from_north, columns), width - 1),
        edge_first,
        edge_second,
    )
    ends = [moved(air, sides, 0), moved(air, sides, rows - 1), edge]
    joined = jnp.concatenate(ends, axis=1)
    joined = joined + physics_rate * jnp.tanh(tendency(*split(joined)))
    mid[1] = joined[:, :width]
    mid[rows] = joined[:, width : 2 * width]
    rows_out[2] = joined[:, :width].astype(bf16)
    rows_out[3] = joined[:, width : 2 * width].astype(bf16)
    edge_out[1] = joined[:, 2 * width :].astype(bf16)
    second_halo = halo(1)
    for copy in second_halo:
        copy.start()

    def first_move(index, carry):
        value = moved(air, sides, index)
        high, low = split(value)
        mid[index + 1] = value
        parts[0, index] = high
        parts[1, index] = low
        return carry

    lax.fori_loop(1, rows - 1, first_move, 0, unroll=2)

    def physics_of(field, begin, count):
        high = jnp.concatenate([parts[0, begin + n] for n in range(count)], axis=1)
        low = jnp.concatenate([parts[1, begin + n] for n in range(count)], axis=1)
        change = physics_rate * jnp.tanh(tendency(high, low))
        for n in range(count):
            field[begin + n] = field[begin + n] + change[:, n * width : (n + 1) * width]

    for begin in range(1, rows - 1, 2):
        physics_of(mid.at[pl.ds(1, rows)], begin, 2)

    mid[0] = empty
    mid[rows + 1] = empty

    def second_move(index, carry):
        value = moved(mid, empty, index)
        last[index] = value
        top_ref[pl.ds(index, 1), :] = value[0:1]
        bottom_ref[pl.ds(index, 1), :] = jnp.sum(
            value * physics_top, axis=0, keepdims=True
        )
        return carry

    lax.fori_loop(0, rows, second_move, 0, unroll=2)

    from_west, from_east, from_south, from_north = arrive(1, second_halo)
    west_term = from_west * (
        jnp.maximum(wind[0, 0].astype(f32), 0.0) + diffusion_rate
    )
    east_term = from_east * (
        diffusion_rate - jnp.minimum(wind[0, rows - 1].astype(f32), 0.0)
    )
    side_term = jnp.where(
        spot == 2,
        turn(from_south, 1) * (jnp.maximum(edge_second, 0.0) + diffusion_rate),
        turn(from_north, width - 1) * (diffusion_rate - jnp.minimum(edge_second, 0.0)),
    )

    def summed(value):
        return jnp.sum(value * physics_top, axis=0, keepdims=True)

    first_row, last_row = sub_x == 0, sub_x == rows - 1

    def with_terms(value, west_row, east_row, side_row):
        value = value + jnp.where(first_row, west_row, 0.0)
        value = value + jnp.where(last_row, east_row, 0.0)
        for lane_at, spot_at in ((0, 2), (width - 1, 1)):
            term = jnp.sum(
                jnp.where(lane_x == 4 * sub_x + 4 + spot_at, side_row, 0.0),
                axis=1,
                keepdims=True,
            )
            value = value + jnp.where(lane_x == lane_at, term, 0.0)
        return value

    bottom_tendency = with_terms(
        bottom_ref[...], summed(west_term), summed(east_term), summed(side_term)
    )
    bottom = with_terms(
        top_ref[...], west_term[0:1], east_term[0:1], side_term[0:1]
    ) + physics_rate * jnp.tanh(bottom_tendency)
    heat_share = folded(exchange_speed * (bottom - heat_offset))
    share = jnp.where((lane_x // WIDE) % 2 == 0, heat_share, solar_share)
    share_parts = []
    for part in split(share):
        share_parts += two_halves(part.astype(f32), lane_x // (2 * WIDE))
    flux = dot(placing, jnp.concatenate(share_parts, axis=0).astype(bf16))
    flux_out[...] = flux.reshape(PEERS, 1, width)
    flux_in[pl.ds(0, 1)] = flux[0:1].reshape(1, 1, width)
    swap(flux_out, flux_in, 1, 1)

    whole(info_out, info_in, 0).wait_recv()
    tiles_in = info_in[...].reshape(PEERS, width)
    eight = (8, width)
    lane_8, sub_8 = lanes(eight), subs(eight)
    tiles_row = jnp.sum(
        jnp.where(lane_p % WIDE == sub_p, tiles_in, 0.0), axis=0, keepdims=True
    )
    adding = jnp.concatenate(
        [
            jnp.where(
                tiles_row == (4 * sub_8 + 2 * part + lane_8 // (2 * WIDE) + 1).astype(f32),
                1.0,
                0.0,
            )
            for part in range(2)
        ],
        axis=1,
    ).astype(bf16)
    inner = lane_p % WIDE
    reading = jnp.where(
        tiles_in == (4 * (inner % 8) + inner // 8 + 1).astype(f32), 1.0, 0.0
    ).astype(bf16)

    last[0] = last[0] + west_term
    last[rows - 1] = last[rows - 1] + east_term
    fringe_lane = (lane == 0) | (lane == width - 1)

    def settle(index, carry):
        fringe = turn(side_term, width - (4 * index + 6))
        value = last[index] + jnp.where(fringe_lane, fringe, 0.0)
        high, low = split(value)
        last[index] = value
        parts[0, index] = high
        parts[1, index] = low
        return carry

    lax.fori_loop(0, rows, settle, 0, unroll=2)
    for begin in range(0, rows, 2):
        physics_of(last, begin, 2)
    store_air = pltpu.make_async_copy(last, air_out, store_sem.at[0])
    store_air.start()

    whole(flux_out, flux_in, 1).wait_recv()
    shares_in = flux_in[...].reshape(PEERS, width)
    turned = [turn(shares_in, step * WIDE) if step else shares_in for step in range(4)]
    group_p = lane_p // WIDE
    stacked = []
    for place in range(4):
        here = group_p == place
        for slot in range(2):
            stacked.append(
                jnp.concatenate(
                    [
                        jnp.where(here, turned[(place - 2 * slot - kind) % 4], 0.0)
                        for kind in range(2)
                    ],
                    axis=1,
                )
            )
    stacked = jnp.concatenate(stacked, axis=0)
    stacked_high, stacked_low = split(stacked)
    forcing = dot(adding, stacked_high) + dot(adding, stacked_low)
    heat_in, solar_in = forcing[:, :width], forcing[:, width:]
    top = base_top[...] + solar_gain[0:1] * solar_in + heat_gain[0:1] * heat_in
    spread = []
    for place in range(4):
        mine = jnp.where(lane_8 // WIDE == place, top, 0.0)
        mine = mine + turn(mine, WIDE)
        spread.append(mine + turn(mine, 2 * WIDE))
    spread = jnp.concatenate(spread, axis=0)
    spread_lane = lanes((WIDE, width)) // (2 * WIDE)
    read_parts = []
    for part in split(spread):
        for slot in range(2):
            read_parts.append(jnp.where(spread_lane == slot, part.astype(f32), 0.0))
    back = dot(reading, jnp.concatenate(read_parts, axis=0).astype(bf16))
    back_out[...] = back.reshape(PEERS, 1, width)
    back_in[pl.ds(0, 1)] = back[0:1].reshape(1, 1, width)
    swap(back_out, back_in, 2, -1)

    solar_wide = jnp.broadcast_to(solar_gain, (depth, width))
    heat_wide = jnp.broadcast_to(heat_gain, (depth, width))
    for block in range(blocks):
        at = pl.ds(block * width, width)
        ocean[:, at] = (
            base[:, at]
            + solar_wide * solar_in[block : block + 1]
            + heat_wide * heat_in[block : block + 1]
        )
    store_ocean = pltpu.make_async_copy(ocean, ocean_out, store_sem.at[1])
    store_ocean.start()

    whole(back_out, back_in, 2).wait_recv()
    back_now = back_in[...].reshape(PEERS, width)
    back_turned = turn(back_now, 2 * WIDE)
    low_half = lane_p < 2 * WIDE
    served = jnp.concatenate(
        [
            jnp.where(low_half, back_now, back_turned),
            jnp.where(low_half, back_turned, back_now),
        ],
        axis=0,
    )
    served = jnp.concatenate([part.astype(f32) for part in split(served)], axis=0)
    tile_sst = dot(taking, served.astype(bf16))
    tile_sst = jnp.concatenate([tile_sst] * (banks * WIDE // width), axis=1)
    tile_sst = jnp.where(chosen, tile_sst, 0.0)
    sst_high, sst_low = split(tile_sst)
    returned = inverse * (
        dot(sst_high, bank[0]) + dot(sst_high, bank[1]) + dot(sst_low, bank[0])
    )
    surface[...] = fraction * returned + (1.0 - fraction) * bottom
    store_surface = pltpu.make_async_copy(surface, surface_out, store_sem.at[2])
    store_surface.start()

    for copy in first_halo:
        copy.wait_send()
    for copy in second_halo:
        copy.wait_send()
    whole(info_out, info_in, 0).wait_send()
    whole(flux_out, flux_in, 1).wait_send()
    whole(back_out, back_in, 2).wait_send()
    store_air.wait()
    store_ocean.wait()
    store_surface.wait()


def deliver(air_in, ocean_in, surface_in, air_out, ocean_out, surface_out, sems):
    copies = [
        pltpu.make_async_copy(source, target, sems.at[slot])
        for slot, (source, target) in enumerate(
            ((air_in, air_out), (ocean_in, ocean_out), (surface_in, surface_out))
        )
    ]
    for copy in copies:
        copy.start()
    for copy in copies:
        copy.wait()


def local(groups, rings, *operands):
    route = operands[6]
    operands = operands[:6] + (route.reshape(route.shape[:2]),) + operands[7:]
    air_temp, remap_tiles, ocean_temp = operands[0], operands[9], operands[10]
    rows, levels, width = air_temp.shape
    banks = remap_tiles.shape[0]
    depth = ocean_temp.shape[0]
    anywhere = pl.BlockSpec(memory_space=pl.ANY)
    pinned = pl.BlockSpec(memory_space=pltpu.HBM)
    message = pltpu.VMEM((PEERS, 1, width), f32)
    results = pl.pallas_call(
        functools.partial(kernel, groups, rings),
        out_shape=(
            jax.ShapeDtypeStruct(air_temp.shape, f32),
            jax.ShapeDtypeStruct(ocean_temp.shape, f32),
            jax.ShapeDtypeStruct((rows, width), f32),
        ),
        in_specs=[pinned] * 12,
        out_specs=(anywhere, anywhere, anywhere),
        scratch_shapes=[
            pltpu.VMEM((rows + 2, levels, width), f32),
            pltpu.VMEM((rows + 2, levels, width), f32),
            pltpu.VMEM((rows, levels, width), f32),
            pltpu.VMEM((2, rows, levels, width), bf16),
            pltpu.VMEM((2, rows, levels, width), bf16),
            pltpu.VMEM(ocean_temp.shape, f32),
            pltpu.VMEM(ocean_temp.shape, f32),
            pltpu.VMEM((8, width), f32),
            pltpu.VMEM((2, banks * WIDE, width), bf16),
            pltpu.VMEM((2, width, banks * WIDE), bf16),
            pltpu.VMEM((rows, width), f32),
            pltpu.VMEM((rows, width), f32),
            pltpu.VMEM((rows, width), f32),
            pltpu.VMEM((rows, width), f32),
            pltpu.VMEM((4, levels, width), bf16),
            pltpu.VMEM((4, levels, width), bf16),
            pltpu.VMEM((2, levels, width), bf16),
            pltpu.VMEM((4, levels, width), bf16),
        ]
        + [message] * 6
        + [
            pltpu.VMEM(operand.shape, operand.dtype)
            for operand in operands[2:10] + operands[11:]
        ]
        + [
            pltpu.SemaphoreType.DMA((12,)),
            pltpu.SemaphoreType.DMA((3,)),
            pltpu.SemaphoreType.DMA((8,)),
            pltpu.SemaphoreType.DMA((8,)),
            pltpu.SemaphoreType.DMA((3,)),
            pltpu.SemaphoreType.DMA((3,)),
        ],
        compiler_params=pltpu.CompilerParams(
            collective_id=0, has_side_effects=True, vmem_limit_bytes=48 * 1024 * 1024
        ),
    )(*[pltpu.with_memory_space_constraint(each, pltpu.HBM) for each in operands])
    return pl.pallas_call(
        deliver,
        out_shape=tuple(jax.ShapeDtypeStruct(each.shape, each.dtype) for each in results),
        in_specs=[anywhere] * 3,
        out_specs=(pinned,) * 3,
        scratch_shapes=[pltpu.SemaphoreType.DMA((3,))],
        compiler_params=pltpu.CompilerParams(vmem_limit_bytes=4 * 1024 * 1024),
    )(*results)


def solution(mesh):
    placed = (
        P("atm", None, "cpl"),
        P(None, "atm", None, "cpl"),
        P(),
        P("atm", "cpl"),
        P("atm", "cpl"),
        P("atm", "cpl"),
        P("cpl", "atm", None),
        P("cpl", "atm"),
        P("cpl", "atm"),
        P(),
        P(None, ("atm", "cpl")),
        P(),
    )
    return jax.shard_map(
        functools.partial(local, mesh.shape["cpl"], mesh.shape["atm"]),
        mesh=mesh,
        in_specs=placed,
        out_specs=(P("atm", None, "cpl"), P(None, ("atm", "cpl")), P("atm", "cpl")),
        check_vma=False,
    )
```

```python
import functools
import math

import jax
import jax.numpy as jnp
from jax import lax
from jax.experimental import pallas as pl
from jax.experimental.pallas import tpu as pltpu
from jax.sharding import PartitionSpec as P

diffusion_rate = 0.05
physics_rate = 0.5
f32 = jnp.float32
bf16 = jnp.bfloat16
PEERS = 32
WIDE = 32


def split(value):
    high = value.astype(bf16)
    return high, (value - high.astype(f32)).astype(bf16)


def lanes(shape):
    return lax.broadcasted_iota(jnp.int32, shape, len(shape) - 1)


def subs(shape):
    return lax.broadcasted_iota(jnp.int32, shape, len(shape) - 2)


def dot(left, right):
    return jnp.dot(left, right, preferred_element_type=f32)


def dot3(left_parts, right_parts):
    return (
        dot(left_parts[0], right_parts[0])
        + dot(left_parts[0], right_parts[1])
        + dot(left_parts[1], right_parts[0])
    )


def turn(value, shift):
    return pltpu.roll(value, shift, len(value.shape) - 1)


def transport(center, west, east, south, north, first, second):
    first_up = jnp.maximum(first, 0.0)
    first_down = first - first_up
    second_up = jnp.maximum(second, 0.0)
    second_down = second - second_up
    keep = (1.0 - 4.0 * diffusion_rate) - (first_up - first_down) - (second_up - second_down)
    return (
        center * keep
        + west * (first_up + diffusion_rate)
        + east * (diffusion_rate - first_down)
        + south * (second_up + diffusion_rate)
        + north * (diffusion_rate - second_down)
    )


def kernel(
    groups,
    rings,
    air_hbm,
    wind_hbm,
    physics_hbm,
    sea_hbm,
    short_hbm,
    mask_hbm,
    route_hbm,
    tile_hbm,
    weight_hbm,
    remap_hbm,
    ocean_hbm,
    mixing_hbm,
    air_out,
    ocean_out,
    surface_out,
    air,
    mid,
    last,
    wind,
    parts,
    ocean,
    base,
    bank,
    bank_turned,
    bottom_ref,
    gust_ref,
    top_ref,
    surface,
    rows_out,
    rows_in,
    edge_out,
    edge_in,
    early_out,
    early_in,
    flux_out,
    flux_in,
    physics_ref,
    sea_ref,
    short_ref,
    mask_ref,
    route_ref,
    tile_ref,
    weight_ref,
    remap_ref,
    mixing_ref,
    load_sem,
    store_sem,
    halo_send,
    halo_recv,
    swap_send,
    swap_recv,
):
    rows, levels, width = air_hbm.shape[0], air_hbm.shape[1], air_hbm.shape[2]
    depth = ocean_hbm.shape[0]
    blocks = ocean_hbm.shape[1] // width
    banks = remap_hbm.shape[0]
    atm, cpl = lax.axis_index("atm"), lax.axis_index("cpl")
    west = lax.rem(atm + rings - 1, rings)
    east = lax.rem(atm + 1, rings)
    south = lax.rem(cpl + groups - 1, groups)
    north = lax.rem(cpl + 1, groups)

    barrier = pltpu.get_barrier_semaphore()
    for near in (west, east):
        pl.semaphore_signal(barrier, inc=1, device_id={"atm": near, "cpl": cpl})

    pairs = (
        (air_hbm, air.at[pl.ds(1, rows)]),
        (wind_hbm, wind),
        (route_hbm, route_ref),
        (tile_hbm, tile_ref),
        (weight_hbm, weight_ref),
        (remap_hbm, remap_ref),
        (physics_hbm, physics_ref),
        (mask_hbm, mask_ref),
        (short_hbm, short_ref),
        (sea_hbm, sea_ref),
        (mixing_hbm, mixing_ref),
        (ocean_hbm, ocean),
    )
    loads = [
        pltpu.make_async_copy(source, target, load_sem.at[slot])
        for slot, (source, target) in enumerate(pairs)
    ]
    loads[0].start()

    def far_first(turn_at):
        return groups // 2 + (1 - 2 * (turn_at % 2)) * ((turn_at + 1) // 2)

    def greet(turn_at, carry):
        peer_at = lax.rem(cpl + far_first(turn_at), groups)
        pl.semaphore_signal(barrier, inc=1, device_id={"atm": atm, "cpl": peer_at})
        return carry

    lax.fori_loop(0, groups - 1, greet, 0)
    for load in loads[1:]:
        load.start()

    if groups < PEERS:
        for unused in (early_in, flux_in):
            unused[pl.ds(groups, PEERS - groups)] = jnp.zeros(
                (PEERS - groups,) + unused.shape[1:], unused.dtype
            )

    sheet = (levels, width)
    lane = lanes(sheet)
    spot = lane % 4
    owner_lane = lane // 4

    loads[0].wait()
    rows_out[0] = air[1].astype(bf16)
    rows_out[1] = air[rows].astype(bf16)

    def gather(index, columns):
        here = turn(air[index + 1], 4 * index + 6)
        return jnp.where(owner_lane == index + 1, here, columns)

    empty = jnp.zeros(sheet, f32)
    columns = lax.fori_loop(0, rows, gather, empty, unroll=8)
    edge_out[0] = columns.astype(bf16)

    pl.semaphore_wait(barrier, groups + 1)

    def ring(source, target, slot, device):
        return pltpu.make_async_remote_copy(
            src_ref=source,
            dst_ref=target,
            send_sem=halo_send.at[slot],
            recv_sem=halo_recv.at[slot],
            device_id=device,
        )

    def halo(phase):
        copies = (
            ring(
                rows_out.at[2 * phase],
                rows_in.at[2 * phase],
                4 * phase,
                {"atm": west, "cpl": cpl},
            ),
            ring(
                rows_out.at[2 * phase + 1],
                rows_in.at[2 * phase + 1],
                4 * phase + 1,
                {"atm": east, "cpl": cpl},
            ),
            ring(
                edge_out.at[phase],
                edge_in.at[2 * phase],
                4 * phase + 2,
                {"atm": atm, "cpl": south},
            ),
            ring(
                edge_out.at[phase],
                edge_in.at[2 * phase + 1],
                4 * phase + 3,
                {"atm": atm, "cpl": north},
            ),
        )
        return copies

    def swap(source, target, slot):
        def send(turn_at, carry):
            step = far_first(turn_at)
            device = lax.rem(cpl + step, groups)
            pltpu.make_async_remote_copy(
                src_ref=source,
                dst_ref=target.at[step],
                send_sem=swap_send.at[slot],
                recv_sem=swap_recv.at[slot],
                device_id={"atm": atm, "cpl": device},
            ).start()
            return carry

        lax.fori_loop(0, groups - 1, send, 0)

    def whole(target, slot):
        return pltpu.make_async_remote_copy(
            src_ref=target.at[pl.ds(1, groups - 1)],
            dst_ref=target.at[pl.ds(1, groups - 1)],
            send_sem=swap_send.at[slot],
            recv_sem=swap_recv.at[slot],
            device_id={"atm": atm, "cpl": north},
        )

    first_halo = halo(0)
    for copy in first_halo:
        copy.start()
    for load in loads[2:5]:
        load.wait()
    square = (rows, width)
    lane_x, sub_x = lanes(square), subs(square)
    row_of = lambda ref: jnp.broadcast_to(
        jnp.concatenate(
            [ref[...].astype(f32), jnp.zeros((1, width - rows), f32)], axis=1
        ),
        square,
    )
    column_of = lambda ref: jnp.sum(
        jnp.where(lane_x == sub_x, row_of(ref), 0.0), axis=1, keepdims=True
    )
    route_col = column_of(route_ref)
    me = cpl.astype(f32)
    tile_col = column_of(tile_ref)
    weight_col = column_of(weight_ref)
    key_col = route_col * rows + tile_col
    keys = jnp.concatenate(
        [jnp.broadcast_to(key_col, square), jnp.full((WIDE - rows, width), -1.0, f32)],
        axis=0,
    )
    half = (WIDE // 2, width)
    own_lane = lanes(half) % (WIDE // 2) == subs(half)
    early_out[...] = jnp.zeros_like(early_out)
    for part in range(2):
        early_out[pl.ds(6 + part, 1), :] = jnp.sum(
            jnp.where(own_lane, keys[part * WIDE // 2 : (part + 1) * WIDE // 2], 0.0),
            axis=0,
            keepdims=True,
        )

    loads[1].wait()

    def gather_wind(index, carry):
        first, second = carry
        mine = owner_lane == index + 1
        one = wind[0, index].astype(f32)
        two = wind[1, index].astype(f32)
        first = jnp.where(mine, turn(one, 4 * index + 6), first)
        second = jnp.where(mine, turn(two, 4 * index + 6), second)
        gust_ref[pl.ds(index, 1), :] = one[0:1] * one[0:1] + two[0:1] * two[0:1]
        return first, second

    edge_first, edge_second = lax.fori_loop(
        0, rows, gather_wind, (empty, empty), unroll=4
    )

    for load in loads[5:]:
        load.wait()

    physics_parts = split(physics_ref[...])
    physics_wide = jnp.concatenate(
        [physics_parts[0].astype(f32), physics_parts[1].astype(f32)], axis=1
    ).astype(bf16)

    def tendency(high, low):
        return dot(physics_wide, jnp.concatenate([high, high], axis=0)) + dot(
            physics_parts[0], low
        )

    flat = remap_ref[...].reshape(banks * WIDE, width)
    flat_high, flat_low = split(flat)
    bank[0] = flat_high
    bank[1] = flat_low
    turned_high, turned_low = split(jnp.transpose(flat))
    bank_turned[0] = turned_high
    bank_turned[1] = turned_low
    totals = jnp.sum(remap_ref[...], axis=1)
    bank_lane = lanes((rows, banks * WIDE)) // WIDE
    chosen = bank_lane.astype(f32) == weight_col
    pick = jnp.where(
        lanes((rows, banks)).astype(f32) == weight_col, 1.0, 0.0
    )
    inverse = 1.0 / jnp.dot(
        pick, totals, precision=lax.Precision.HIGHEST, preferred_element_type=f32
    )

    def fold(value):
        value = value + turn(value, WIDE)
        return value + turn(value, 2 * WIDE)

    def folded(flux):
        high, low = split(flux)
        each = (
            dot(high, bank_turned[0]) + dot(low, bank_turned[0]) + dot(high, bank_turned[1])
        )
        each = jnp.where(chosen, each, 0.0)
        total = each[:, :width]
        for part in range(1, banks * WIDE // width):
            total = total + each[:, part * width : (part + 1) * width]
        return fold(total)

    fraction = mask_ref[...].astype(f32)
    solar_share = folded(fraction * short_ref[...])
    exchange_speed = fraction * (0.5 + 2.0 * jnp.sqrt(gust_ref[...] + 0.01))
    heat_offset = sea_ref[...]

    mixing = mixing_ref[...]
    mixing_parts = split(mixing)
    ocean_now = ocean[...]
    base[...] = 0.5 * ocean_now + dot3(mixing_parts, split(ocean_now))
    for block in range(blocks):
        early_out[pl.ds(block, 1), :] = base[pl.ds(0, 1), pl.ds(block * width, width)]
    early_in[0] = early_out[...]
    swap(early_out, early_in, 0)
    scale = 1.0 / sum(math.exp(-level / 8.0) for level in range(depth))
    profile_row = jnp.exp(lanes((depth, depth)).astype(f32) * -0.125) * scale
    profile_col = jnp.exp(subs((depth, 1)).astype(f32) * -0.125) * scale
    solar_gain = 0.5 * profile_col + jnp.sum(mixing * profile_row, axis=1, keepdims=True)
    heat_gain = mixing[:, 0:1] + jnp.where(subs((depth, 1)) == 0, 0.5, 0.0)
    physics_top = jnp.sum(
        jnp.where(
            lanes((levels, levels)) == subs((levels, levels)), physics_ref[0:1, :], 0.0
        ),
        axis=1,
        keepdims=True,
    )
    physics_top = jnp.broadcast_to(physics_top, sheet)

    def moved(field, sides, index):
        center = field[index + 1]
        fringe = turn(sides, width - (4 * index + 6))
        return transport(
            center,
            field[index],
            field[index + 2],
            turn(jnp.where(lane == width - 1, fringe, center), 1),
            turn(jnp.where(lane == 0, fringe, center), width - 1),
            wind[0, index].astype(f32),
            wind[1, index].astype(f32),
        )

    def arrive(phase, copies):
        for copy in copies:
            copy.wait_recv()
        return (
            rows_in[2 * phase + 1].astype(f32),
            rows_in[2 * phase].astype(f32),
            edge_in[2 * phase + 1].astype(f32),
            edge_in[2 * phase].astype(f32),
        )

    from_west, from_east, from_south, from_north = arrive(0, first_halo)
    air[0] = from_west
    air[rows + 1] = from_east
    sides = jnp.where(spot == 1, from_south, from_north)
    columns = jnp.where(owner_lane == 0, turn(air[0], 2), columns)
    columns = jnp.where(
        owner_lane == rows + 1, turn(air[rows + 1], 4 * rows + 6), columns
    )
    edge = transport(
        columns,
        turn(columns, 4),
        turn(columns, width - 4),
        turn(jnp.where(spot == 1, from_south, columns), 1),
        turn(jnp.where(spot == 2, from_north, columns), width - 1),
        edge_first,
        edge_second,
    )
    ends = [moved(air, sides, 0), moved(air, sides, rows - 1), edge]
    joined = jnp.concatenate(ends, axis=1)
    joined = joined + physics_rate * jnp.tanh(tendency(*split(joined)))
    mid[1] = joined[:, :width]
    mid[rows] = joined[:, width : 2 * width]
    rows_out[2] = joined[:, :width].astype(bf16)
    rows_out[3] = joined[:, width : 2 * width].astype(bf16)
    edge_out[1] = joined[:, 2 * width :].astype(bf16)
    second_halo = halo(1)
    for copy in second_halo:
        copy.start()

    def first_move(index, carry):
        value = moved(air, sides, index)
        high, low = split(value)
        mid[index + 1] = value
        parts[0, index] = high
        parts[1, index] = low
        return carry

    lax.fori_loop(1, rows - 1, first_move, 0, unroll=2)

    def physics_of(field, begin, count):
        high = jnp.concatenate([parts[0, begin + n] for n in range(count)], axis=1)
        low = jnp.concatenate([parts[1, begin + n] for n in range(count)], axis=1)
        change = physics_rate * jnp.tanh(tendency(high, low))
        for n in range(count):
            field[begin + n] = field[begin + n] + change[:, n * width : (n + 1) * width]

    for begin in range(1, rows - 1, 2):
        physics_of(mid.at[pl.ds(1, rows)], begin, 2)

    mid[0] = empty
    mid[rows + 1] = empty

    def second_move(index, carry):
        value = moved(mid, empty, index)
        last[index] = value
        top_ref[pl.ds(index, 1), :] = value[0:1]
        bottom_ref[pl.ds(index, 1), :] = jnp.sum(
            value * physics_top, axis=0, keepdims=True
        )
        return carry

    lax.fori_loop(0, rows, second_move, 0, unroll=2)

    from_west, from_east, from_south, from_north = arrive(1, second_halo)
    west_term = from_west * (
        jnp.maximum(wind[0, 0].astype(f32), 0.0) + diffusion_rate
    )
    east_term = from_east * (
        diffusion_rate - jnp.minimum(wind[0, rows - 1].astype(f32), 0.0)
    )
    side_term = jnp.where(
        spot == 2,
        turn(from_south, 1) * (jnp.maximum(edge_second, 0.0) + diffusion_rate),
        turn(from_north, width - 1) * (diffusion_rate - jnp.minimum(edge_second, 0.0)),
    )

    def summed(value):
        return jnp.sum(value * physics_top, axis=0, keepdims=True)

    first_row, last_row = sub_x == 0, sub_x == rows - 1

    def with_terms(value, west_row, east_row, side_row):
        value = value + jnp.where(first_row, west_row, 0.0)
        value = value + jnp.where(last_row, east_row, 0.0)
        for lane_at, spot_at in ((0, 2), (width - 1, 1)):
            term = jnp.sum(
                jnp.where(lane_x == 4 * sub_x + 4 + spot_at, side_row, 0.0),
                axis=1,
                keepdims=True,
            )
            value = value + jnp.where(lane_x == lane_at, term, 0.0)
        return value

    bottom_tendency = with_terms(
        bottom_ref[...], summed(west_term), summed(east_term), summed(side_term)
    )
    bottom = with_terms(
        top_ref[...], west_term[0:1], east_term[0:1], side_term[0:1]
    ) + physics_rate * jnp.tanh(bottom_tendency)
    heat_share = folded(exchange_speed * (bottom - heat_offset))
    share = jnp.where((lane_x // WIDE) % 2 == 0, heat_share, solar_share)
    share = jnp.concatenate([share, jnp.zeros((WIDE - rows, width), f32)], axis=0)
    flux = jnp.where(
        lanes(half) < 2 * WIDE, share[: WIDE // 2], share[WIDE // 2 :]
    ).astype(bf16)
    flux_out[...] = flux
    flux_in[0] = flux
    swap(flux_out, flux_in, 1)

    whole(early_in, 0).wait_recv()
    early = early_in[...].reshape(PEERS * 8, width)
    place_col = jnp.floor(tile_col * 0.25)
    slot_col = me - route_col
    slot_col = jnp.where(slot_col < 0.0, slot_col + groups, slot_col)
    reading = jnp.where(
        lanes((rows, PEERS * 8)).astype(f32) == slot_col * 8 + place_col, 1.0, 0.0
    ).astype(bf16)
    early_high, early_low = split(early)
    tile_base = dot(reading, early_high) + dot(reading, early_low)
    group_x = (lane_x // WIDE).astype(f32)
    tile_base = fold(jnp.where(group_x == tile_col - 4.0 * place_col, tile_base, 0.0))
    early_row, early_lane = subs(early.shape), lanes(early.shape)
    inner = subs((WIDE, 1))
    own_tile = 4 * (inner % 8) + inner // 8
    own_key = jnp.where(own_tile < rows, (own_tile + cpl * rows).astype(f32), -2.0)
    all_keys = jnp.concatenate([key_col, own_key], axis=0)
    meeting = []
    for part in range(2):
        key_rows = [
            jnp.sum(
                jnp.where(
                    early_row == (8 * quarter + early_lane // (WIDE // 2)) * 8 + 6 + part,
                    early,
                    0.0,
                ),
                axis=0,
                keepdims=True,
            )
            for quarter in range(4)
        ]
        meeting.append(
            jnp.where(all_keys == jnp.concatenate(key_rows, axis=1), 1.0, 0.0)
        )
    meeting = jnp.concatenate(meeting, axis=0).astype(bf16)

    last[0] = last[0] + west_term
    last[rows - 1] = last[rows - 1] + east_term
    fringe_lane = (lane == 0) | (lane == width - 1)

    def settle(index, carry):
        fringe = turn(side_term, width - (4 * index + 6))
        value = last[index] + jnp.where(fringe_lane, fringe, 0.0)
        high, low = split(value)
        last[index] = value
        parts[0, index] = high
        parts[1, index] = low
        return carry

    lax.fori_loop(0, rows, settle, 0, unroll=2)
    for begin in range(0, rows, 2):
        physics_of(last, begin, 2)
    store_air = pltpu.make_async_copy(last, air_out, store_sem.at[0])
    store_air.start()

    whole(flux_in, 1).wait_recv()
    met = dot(meeting, flux_in[...].reshape(PEERS * WIDE // 2, width))
    met = met[: rows + WIDE] + turn(met[rows + WIDE :], 2 * WIDE)
    mine = met[:rows]
    gain = jnp.where(
        lane_x < WIDE, heat_gain[0:1], jnp.where(lane_x < 2 * WIDE, solar_gain[0:1], 0.0)
    )
    tile_sst = tile_base + fold(mine * gain)
    tile_sst = jnp.concatenate([tile_sst] * (banks * WIDE // width), axis=1)
    tile_sst = jnp.where(chosen, tile_sst, 0.0)
    sst_high, sst_low = split(tile_sst)
    returned = inverse * (
        dot(sst_high, bank[0]) + dot(sst_high, bank[1]) + dot(sst_low, bank[0])
    )
    surface[...] = fraction * returned + (1.0 - fraction) * bottom
    store_surface = pltpu.make_async_copy(surface, surface_out, store_sem.at[2])
    store_surface.start()

    group_8 = lanes((8, width)) // WIDE
    heat_in = jnp.zeros((8, width), f32)
    solar_in = heat_in
    for place in range(4):
        block = met[rows + 8 * place : rows + 8 * place + 8]
        here = group_8 == place
        heat_in = heat_in + jnp.where(here, turn(block, place * WIDE), 0.0)
        solar_in = solar_in + jnp.where(here, turn(block, (place + 3) % 4 * WIDE), 0.0)
    solar_wide = jnp.broadcast_to(solar_gain, (depth, width))
    heat_wide = jnp.broadcast_to(heat_gain, (depth, width))
    for block in range(blocks):
        at = pl.ds(block * width, width)
        ocean[:, at] = (
            base[:, at]
            + solar_wide * solar_in[block : block + 1]
            + heat_wide * heat_in[block : block + 1]
        )
    store_ocean = pltpu.make_async_copy(ocean, ocean_out, store_sem.at[1])
    store_ocean.start()

    for copy in first_halo:
        copy.wait_send()
    for copy in second_halo:
        copy.wait_send()
    whole(early_in, 0).wait_send()
    whole(flux_in, 1).wait_send()
    store_air.wait()
    store_ocean.wait()
    store_surface.wait()


def deliver(air_in, ocean_in, surface_in, air_out, ocean_out, surface_out, sems):
    copies = [
        pltpu.make_async_copy(source, target, sems.at[slot])
        for slot, (source, target) in enumerate(
            ((air_in, air_out), (ocean_in, ocean_out), (surface_in, surface_out))
        )
    ]
    for copy in copies:
        copy.start()
    for copy in copies:
        copy.wait()


def local(groups, rings, *operands):
    route = operands[6]
    operands = operands[:6] + (route.reshape(route.shape[:2]),) + operands[7:]
    air_temp, remap_tiles, ocean_temp = operands[0], operands[9], operands[10]
    rows, levels, width = air_temp.shape
    banks = remap_tiles.shape[0]
    depth = ocean_temp.shape[0]
    anywhere = pl.BlockSpec(memory_space=pl.ANY)
    pinned = pl.BlockSpec(memory_space=pltpu.HBM)
    results = pl.pallas_call(
        functools.partial(kernel, groups, rings),
        out_shape=(
            jax.ShapeDtypeStruct(air_temp.shape, f32),
            jax.ShapeDtypeStruct(ocean_temp.shape, f32),
            jax.ShapeDtypeStruct((rows, width), f32),
        ),
        in_specs=[pinned] * 12,
        out_specs=(anywhere, anywhere, anywhere),
        scratch_shapes=[
            pltpu.VMEM((rows + 2, levels, width), f32),
            pltpu.VMEM((rows + 2, levels, width), f32),
            pltpu.VMEM((rows, levels, width), f32),
            pltpu.VMEM((2, rows, levels, width), bf16),
            pltpu.VMEM((2, rows, levels, width), bf16),
            pltpu.VMEM(ocean_temp.shape, f32),
            pltpu.VMEM(ocean_temp.shape, f32),
            pltpu.VMEM((2, banks * WIDE, width), bf16),
            pltpu.VMEM((2, width, banks * WIDE), bf16),
            pltpu.VMEM((rows, width), f32),
            pltpu.VMEM((rows, width), f32),
            pltpu.VMEM((rows, width), f32),
            pltpu.VMEM((rows, width), f32),
            pltpu.VMEM((4, levels, width), bf16),
            pltpu.VMEM((4, levels, width), bf16),
            pltpu.VMEM((2, levels, width), bf16),
            pltpu.VMEM((4, levels, width), bf16),
        ]
        + [
            pltpu.VMEM((8, width), f32),
            pltpu.VMEM((PEERS, 8, width), f32),
            pltpu.VMEM((WIDE // 2, width), bf16),
            pltpu.VMEM((PEERS, WIDE // 2, width), bf16),
        ]
        + [
            pltpu.VMEM(operand.shape, operand.dtype)
            for operand in operands[2:10] + operands[11:]
        ]
        + [
            pltpu.SemaphoreType.DMA((12,)),
            pltpu.SemaphoreType.DMA((3,)),
            pltpu.SemaphoreType.DMA((8,)),
            pltpu.SemaphoreType.DMA((8,)),
            pltpu.SemaphoreType.DMA((2,)),
            pltpu.SemaphoreType.DMA((2,)),
        ],
        compiler_params=pltpu.CompilerParams(
            collective_id=0, has_side_effects=True, vmem_limit_bytes=48 * 1024 * 1024
        ),
    )(*[pltpu.with_memory_space_constraint(each, pltpu.HBM) for each in operands])
    return pl.pallas_call(
        deliver,
        out_shape=tuple(jax.ShapeDtypeStruct(each.shape, each.dtype) for each in results),
        in_specs=[anywhere] * 3,
        out_specs=(pinned,) * 3,
        scratch_shapes=[pltpu.SemaphoreType.DMA((3,))],
        compiler_params=pltpu.CompilerParams(vmem_limit_bytes=4 * 1024 * 1024),
    )(*results)


def solution(mesh):
    placed = (
        P("atm", None, "cpl"),
        P(None, "atm", None, "cpl"),
        P(),
        P("atm", "cpl"),
        P("atm", "cpl"),
        P("atm", "cpl"),
        P("cpl", "atm", None),
        P("cpl", "atm"),
        P("cpl", "atm"),
        P(),
        P(None, ("atm", "cpl")),
        P(),
    )
    return jax.shard_map(
        functools.partial(local, mesh.shape["cpl"], mesh.shape["atm"]),
        mesh=mesh,
        in_specs=placed,
        out_specs=(P("atm", None, "cpl"), P(None, ("atm", "cpl")), P("atm", "cpl")),
        check_vma=False,
    )
```
